128 devices in a mesh: tm: 16 (over z_hi, y, core), space: 8 (over x, z_lo).
Axes of the slice: x: 4, y: 4, z: 4 (z_hi: 2, z_lo: 2; z = z_hi * 2 + z_lo), core: 2. Of those that a mesh axis runs over, the one named last changes fastest.
Arguments:
- tokens: bfloat16 [64, 24, 80, 1024], P('tm', 'space'), may hold values from -6 to 6
- w_in: bfloat16 [1024, 4416], replicated, may hold values from -0.1875 to 0.1875
- w_out: bfloat16 [2048, 1024], replicated, may hold values from -0.125 to 0.125
- a_log_time: float32 [32], replicated, may hold values from -16 to -3
- a_log_space: float32 [32], replicated, may hold values from -14 to -3
- dt_bias_time: float32 [32], replicated, may hold values from -1 to 1
- dt_bias_space: float32 [32], replicated, may hold values from -1 to 1
- skip_time: float32 [32], replicated, may hold values from 0.5 to 1.5
- skip_space: float32 [32], replicated, may hold values from 0.5 to 1.5
- norm_gain: float32 [2048], replicated, may hold values from 0.25 to 1.75
Outputs:
- mixed: bfloat16 [64, 24, 80, 1024], P('tm', 'space')
The draws below stay inside these ranges and needn't reach their ends.
All inputs are finite; a program needn't handle non-finite values.
Results may differ from the reference program's by a relative error of at most 0.0062.
The reference program's roundings to bfloat16 on the way count: a program that leaves them out, or rounds other values in their place, can miss the bound.
Values may be sent and summed in bfloat16 or wider, within the bound.
A program may use at most 192 MiB of HBM per device.

```python
import jax
import jax.numpy as jnp
from jax import lax

D = 1024
HEADS = 32
HEAD_DIM = 64
STATE = 64
COLS = 80
DI = 2048
NPROJ = 4416
FRAMES = 64
ROWS = 24


def level_of(own_key, extent, pieces, smallest, high):
    factor_of = 1.0
    for position, shards_of in pieces:
        heights = jax.random.uniform(jax.random.fold_in(jax.random.fold_in(own_key, 6), position), (shards_of,), jnp.float32, smallest / len(pieces), high / len(pieces))
        factor_of = factor_of * jnp.repeat(jnp.exp(heights), extent[position] // shards_of).reshape((-1,) + (1,) * (len(extent) - 1 - position))
    return factor_of


def noise(own_key, dims, scale, bound, cuts=(), kind=jnp.bfloat16):
    drawn = scale * jax.random.normal(own_key, dims, jnp.float32)
    if cuts:
        drawn = drawn * level_of(own_key, dims, cuts, -0.22, 0.18)
    return jnp.clip(drawn, -bound, bound).astype(kind)


def setup_inputs(seed: int = 0) -> dict:
    streams_of = jax.random.split(jax.random.key(seed), 11)
    tokens = noise(streams_of[0], (FRAMES, ROWS, COLS, D), 1.0, 6.0, ((0, 16), (1, 8)))
    w_in = noise(streams_of[1], (D, NPROJ), D ** -0.5, 0.1875)
    w_out = noise(streams_of[2], (DI, D), DI ** -0.5, 0.125)
    a_log_time = jnp.clip(jax.random.uniform(streams_of[3], (HEADS,), jnp.float32, -16.0, -3.0), -16.0, -3.0)
    a_log_space = jnp.clip(jax.random.uniform(streams_of[4], (HEADS,), jnp.float32, -14.0, -3.0), -14.0, -3.0)
    dt_bias_time = jnp.clip(jax.random.uniform(streams_of[5], (HEADS,), jnp.float32, -1.0, 1.0), -1.0, 1.0)
    dt_bias_space = jnp.clip(jax.random.uniform(streams_of[6], (HEADS,), jnp.float32, -1.0, 1.0), -1.0, 1.0)
    skip_time = jnp.clip(jax.random.uniform(streams_of[7], (HEADS,), jnp.float32, 0.5, 1.5), 0.5, 1.5)
    skip_space = jnp.clip(jax.random.uniform(streams_of[8], (HEADS,), jnp.float32, 0.5, 1.5), 0.5, 1.5)
    norm_gain = jnp.clip(1.0 + 0.15 * jax.random.normal(streams_of[9], (DI,), jnp.float32), 0.25, 1.75)
    return {"tokens": tokens, "w_in": w_in, "w_out": w_out, "a_log_time": a_log_time, "a_log_space": a_log_space, "dt_bias_time": dt_bias_time, "dt_bias_space": dt_bias_space, "skip_time": skip_time, "skip_space": skip_space, "norm_gain": norm_gain}


def split_pieces(projected):
    base = 2 * DI
    gate_z = projected[:, :DI].astype(jnp.bfloat16)
    inner_x = projected[:, DI:base].astype(jnp.bfloat16)
    b_time = projected[:, base:base + STATE].astype(jnp.bfloat16)
    c_time = projected[:, base + STATE:base + 2 * STATE].astype(jnp.bfloat16)
    b_space = projected[:, base + 2 * STATE:base + 3 * STATE].astype(jnp.bfloat16)
    c_space = projected[:, base + 3 * STATE:base + 4 * STATE].astype(jnp.bfloat16)
    raw_time = projected[:, base + 4 * STATE:base + 4 * STATE + HEADS].astype(jnp.bfloat16)
    raw_space = projected[:, base + 4 * STATE + HEADS:base + 4 * STATE + 2 * HEADS]
    return (gate_z, inner_x, b_time, c_time, b_space, c_space, raw_time, raw_space)

def local_scan(inner_seq, inject, readout, log_decay, step_size):
    signal = inner_seq.astype(jnp.float32)
    inject_wide = inject.astype(jnp.float32)
    readout_wide = readout.astype(jnp.float32)
    cum_decay = jnp.cumsum(log_decay, axis=0)
    scores = jnp.dot(readout_wide, inject_wide.T, precision=lax.Precision.HIGHEST)
    log_span = cum_decay[:, None, :] - cum_decay[None, :, :]
    length = log_decay.shape[0]
    causal = jnp.arange(length)[:, None] >= jnp.arange(length)[None, :]
    decay_mask = jnp.where(causal[:, :, None], jnp.exp(jnp.minimum(log_span, 0.0)), 0.0)
    weights = decay_mask * scores[:, :, None] * step_size[None, :, :]
    local_out = jnp.einsum('srh,rhp->shp', weights, signal, precision=lax.Precision.HIGHEST)
    tail_weight = jnp.exp(cum_decay[-1][None, :] - cum_decay) * step_size
    end_state = jnp.einsum('rhp,rn->hpn', tail_weight[:, :, None] * signal, inject_wide, precision=lax.Precision.HIGHEST)
    return (local_out, end_state, cum_decay[-1], cum_decay)

def apply_start(local_out, cum_decay, readout, inner_seq, skip_gain, start_state):
    carried = jnp.einsum('sn,hpn->shp', readout.astype(jnp.float32), start_state, precision=lax.Precision.HIGHEST)
    return local_out + jnp.exp(cum_decay)[:, :, None] * carried + skip_gain[None, :, None] * inner_seq.astype(jnp.float32)

def stretch_full(inner_seq, inject, readout, log_decay, step_size, skip_gain, start_state):
    local_out, end_state, total_decay, cum_decay = local_scan(inner_seq, inject, readout, log_decay, step_size)
    result = apply_start(local_out, cum_decay, readout, inner_seq, skip_gain, start_state)
    return (result, jnp.exp(total_decay)[:, None, None] * start_state + end_state)

def reference(tokens, w_in, w_out, a_log_time, a_log_space, dt_bias_time, dt_bias_space, skip_time, skip_space, norm_gain):

    def project_frame(frame_tok):
        projected = jnp.dot(frame_tok.reshape(-1, D), w_in, preferred_element_type=jnp.float32)
        return split_pieces(projected)
    gate_z, inner_x, b_time, c_time, b_space, c_space, raw_time, raw_space = lax.map(project_frame, tokens)
    step_time = jax.nn.softplus(raw_time.astype(jnp.float32) + dt_bias_time)
    step_space = jax.nn.softplus(raw_space + dt_bias_space)
    decay_time = -jnp.exp(a_log_time) * step_time
    decay_space = -jnp.exp(a_log_space) * step_space

    def on_grid(values):
        return values.reshape((FRAMES, ROWS, COLS) + values.shape[2:])

    def by_rows(values):
        return jnp.swapaxes(values, 0, 1)
    inner_grid = inner_x.reshape(FRAMES, ROWS, COLS, HEADS, HEAD_DIM)
    run_rows = jax.vmap(stretch_full, in_axes=(0, 0, 0, 0, 0, None, 0))

    def time_row(row_in):
        reordered = [jnp.swapaxes(values, 0, 1) for values in row_in]
        zero_start = jnp.zeros((COLS, HEADS, HEAD_DIM, STATE), jnp.float32)
        result, unused_end = run_rows(reordered[0], reordered[1], reordered[2], reordered[3], reordered[4], skip_time, zero_start)
        return jnp.swapaxes(result.astype(jnp.bfloat16), 0, 1)
    time_rows = lax.map(time_row, (by_rows(inner_grid), by_rows(on_grid(b_time)), by_rows(on_grid(c_time)), by_rows(on_grid(decay_time)), by_rows(on_grid(step_time))))

    def space_step(carried_state, row_in):
        inner_seq, inject, readout, log_decay, step_size, gate_row = row_in
        result, next_state = run_rows(inner_seq, inject, readout, log_decay, step_size, skip_space, carried_state)
        gated = result.reshape(FRAMES, COLS, DI) * jax.nn.silu(gate_row.astype(jnp.float32))
        inv_scale = lax.rsqrt(lax.optimization_barrier(jnp.mean(gated * gated, axis=-1, keepdims=True)) + 1e-05)
        return (next_state, (gated * inv_scale * norm_gain).astype(jnp.bfloat16))
    space_init = jnp.zeros((FRAMES, HEADS, HEAD_DIM, STATE), jnp.float32)
    unused_last, normed = lax.scan(space_step, space_init, (time_rows, by_rows(on_grid(b_space)), by_rows(on_grid(c_space)), by_rows(on_grid(decay_space)), by_rows(on_grid(step_space)), by_rows(on_grid(gate_z))))
    normed = jnp.swapaxes(normed, 0, 1)

    def finish_frame(frame_in):
        normed_frame, token_frame = frame_in
        summed = jnp.dot(normed_frame.reshape(-1, DI), w_out, preferred_element_type=jnp.float32)
        summed = summed + token_frame.reshape(-1, D).astype(jnp.float32)
        return summed.astype(jnp.bfloat16).reshape(ROWS, COLS, D)
    return lax.map(finish_frame, (normed, tokens))
```

```python
import functools

import jax
import jax.numpy as jnp
from jax import lax
from jax.experimental import pallas as pl
from jax.experimental.pallas import tpu as pltpu
from jax.sharding import PartitionSpec as P

D = 1024
HEADS = 32
HEAD_DIM = 64
STATE = 64
DI = 2048
CHUNK = 64
F32 = jnp.float32
BF16 = jnp.bfloat16
MIB = 1 << 20


def mm(a, b):
    return jnp.dot(a, b, preferred_element_type=F32)


def softplus(v):
    return jnp.maximum(v, 0.0) + jnp.log1p(jnp.exp(-jnp.abs(v)))


def split3(v):
    hi = v.astype(BF16)
    rest = v - hi.astype(F32)
    mid = rest.astype(BF16)
    low = (rest - mid.astype(F32)).astype(BF16)
    return jnp.concatenate([hi, mid, low], axis=1)


def head_spread():
    row = lax.broadcasted_iota(jnp.int32, (3 * HEADS, DI), 0) % HEADS
    col = lax.broadcasted_iota(jnp.int32, (3 * HEADS, DI), 1) // HEAD_DIM
    return (row == col).astype(BF16)


def causal_ones():
    row = lax.broadcasted_iota(jnp.int32, (CHUNK, CHUNK), 0)
    col = lax.broadcasted_iota(jnp.int32, (CHUNK, CHUNK), 1)
    return row >= col


def chunk_cumsum(log_decay):
    tri = causal_ones().astype(F32).astype(BF16)
    wide = mm(tri, split3(log_decay))
    return wide[:, :HEADS] + wide[:, HEADS : 2 * HEADS] + wide[:, 2 * HEADS :]


def row_forms(cum, step):
    pair = jnp.concatenate([cum, step, jnp.zeros((CHUNK, 2 * HEADS), F32)], axis=1)
    return jnp.concatenate([pair, pair], axis=0).T


def pair_rows(turned_ref, base, j, lane_low):
    even = turned_ref[pl.ds(base + 2 * j, 1), :]
    odd = turned_ref[pl.ds(base + 2 * j + 1, 1), :]
    return jnp.where(lane_low, even, odd)


def decay_weights(cum_wide, turned_ref, scores2, j, lane_low):
    cum_row = pair_rows(turned_ref, 0, j, lane_low)
    step_row = pair_rows(turned_ref, HEADS, j, lane_low)
    span = jnp.exp(jnp.minimum(cum_wide - cum_row, 0.0))
    return (span * (scores2 * step_row)).astype(BF16)


def masked_scores(readout, inject):
    scores = lax.dot_general(readout, inject, (((1,), (1,)), ((), ())), preferred_element_type=F32)
    scores = jnp.where(causal_ones(), scores, 0.0)
    return jnp.concatenate([scores, scores], axis=1)


def block_pair(x_pair):
    low = lax.broadcasted_iota(jnp.int32, x_pair.shape, 1) < HEAD_DIM
    zero = jnp.zeros_like(x_pair)
    return jnp.concatenate([jnp.where(low, x_pair, zero), jnp.where(low, zero, x_pair)], axis=0)


def time_kernel(tok_ref, wx_ref, wt_ref, bias_ref, alog_ref, skip_ref, out_ref, spread, x_ref, small_ref, cum_ref, turned):
    items = tok_ref.shape[0] // CHUNK

    @pl.when(pl.program_id(0) == 0)
    def _():
        spread[...] = head_spread()

    tok = tok_ref[...]
    x_ref[...] = mm(tok, wx_ref[...]).astype(BF16)
    small_ref[...] = mm(tok, wt_ref[...]).astype(BF16)
    lane_low = lax.broadcasted_iota(jnp.int32, (1, 2 * CHUNK), 1) < CHUNK
    rate = -jnp.exp(alog_ref[...])

    def item(index, carry):
        rows = pl.ds(pl.multiple_of(index * CHUNK, CHUNK), CHUNK)
        small = small_ref[rows, :]
        scores2 = masked_scores(small[:, STATE : 2 * STATE], small[:, :STATE])
        step = softplus(small[:, 4 * STATE : 4 * STATE + HEADS].astype(F32) + bias_ref[...])
        cum = chunk_cumsum(rate * step)
        turned[...] = row_forms(cum, step)
        cum_ref[...] = mm(split3(cum), spread[...])
        for j in range(HEADS // 2):
            lanes = pl.ds(j * 128, 128)
            weights = decay_weights(cum_ref[:, lanes], turned, scores2, j, lane_low)
            x_pair = x_ref[rows, lanes]
            local = mm(weights, block_pair(x_pair))
            out_ref[rows, lanes] = (local + skip_ref[:, lanes] * x_pair.astype(F32)).astype(BF16)
        return carry

    lax.fori_loop(0, items, item, 0)


def time_scan(tok, w_in, w_tail, bias, alog, skip_wide, per_step):
    rows = per_step * CHUNK
    total = tok.shape[0]
    whole = lambda shape: pl.BlockSpec(shape, lambda i: (0, 0), pipeline_mode=pl.Buffered(1))
    return pl.pallas_call(
        time_kernel,
        out_shape=jax.ShapeDtypeStruct((total, DI), BF16),
        grid=(total // rows,),
        in_specs=[
            pl.BlockSpec((rows, D), lambda i: (i, 0)),
            pl.BlockSpec((D, DI), lambda i: (0, 1), pipeline_mode=pl.Buffered(1)),
            whole(w_tail.shape),
            whole((1, HEADS)),
            whole((1, HEADS)),
            whole((1, DI)),
        ],
        out_specs=pl.BlockSpec((rows, DI), lambda i: (i, 0)),
        scratch_shapes=[
            pltpu.VMEM((3 * HEADS, DI), BF16),
            pltpu.VMEM((rows, DI), BF16),
            pltpu.VMEM((rows, w_tail.shape[1]), BF16),
            pltpu.VMEM((CHUNK, DI), F32),
            pltpu.VMEM((128, 128), F32),
        ],
        compiler_params=pltpu.CompilerParams(vmem_limit_bytes=40 * MIB),
        cost_estimate=pl.CostEstimate(
            flops=2 * total * D * 2400 + 2 * total * 128 * DI,
            bytes_accessed=2 * total * (D + DI) + 2 * D * 2400,
            transcendentals=total * DI,
        ),
    )(tok, w_in, w_tail, bias, alog, skip_wide)


def home_kernel(tok_ref, wz_ref, wt_ref, bias_ref, alog_ref, z_ref, w_ref, small_ref, decay_ref, spread, cum_ref, turned):
    seq = tok_ref.shape[0]

    @pl.when(pl.program_id(0) == 0)
    def _():
        spread[...] = head_spread()

    tok = tok_ref[...]
    z_ref[...] = mm(tok, wz_ref[...]).astype(BF16)
    tail = mm(tok, wt_ref[...])
    inject = tail[:, 2 * STATE : 3 * STATE].astype(BF16)
    readout = tail[:, 3 * STATE : 4 * STATE].astype(BF16)
    step = softplus(tail[:, 4 * STATE + HEADS : 4 * STATE + 2 * HEADS] + bias_ref[...])
    pad = w_ref.shape[0] - seq
    inject = jnp.concatenate([inject, jnp.zeros((pad, STATE), BF16)], axis=0)
    readout = jnp.concatenate([readout, jnp.zeros((pad, STATE), BF16)], axis=0)
    step = jnp.concatenate([step, jnp.zeros((pad, HEADS), F32)], axis=0)
    small_ref[...] = jnp.concatenate([inject, readout], axis=1)
    log_decay = -jnp.exp(alog_ref[...]) * step
    lane_low = lax.broadcasted_iota(jnp.int32, (1, 2 * CHUNK), 1) < CHUNK
    for k in range(w_ref.shape[0] // CHUNK):
        rows = pl.ds(k * CHUNK, CHUNK)
        part = slice(k * CHUNK, (k + 1) * CHUNK)
        cum = chunk_cumsum(log_decay[part])
        decay_ref[rows, :] = jnp.concatenate(
            [cum, step[part], jnp.zeros((CHUNK, 2 * HEADS), F32)], axis=1
        )
        turned[k] = row_forms(cum, step[part])
        cum_ref[...] = mm(split3(cum), spread[...])
        scores2 = masked_scores(readout[part], inject[part])
        for j in range(HEADS // 2):
            lanes = pl.ds(j * 128, 128)
            w_ref[rows, lanes] = decay_weights(cum_ref[:, lanes], turned.at[k], scores2, j, lane_low)


def home_part(tok, w_in, w_tail, bias, alog, frames):
    total = tok.shape[0]
    seq = total // frames
    padded = -(-seq // CHUNK) * CHUNK
    whole = lambda shape: pl.BlockSpec(shape, lambda i: (0, 0), pipeline_mode=pl.Buffered(1))
    row = lambda n, width: pl.BlockSpec((n, width), lambda i: (i, 0))
    return pl.pallas_call(
        home_kernel,
        out_shape=(
            jax.ShapeDtypeStruct((total, DI), BF16),
            jax.ShapeDtypeStruct((frames * padded, DI), BF16),
            jax.ShapeDtypeStruct((frames * padded, 2 * STATE), BF16),
            jax.ShapeDtypeStruct((frames * padded, 128), F32),
        ),
        grid=(frames,),
        in_specs=[
            row(seq, D),
            whole((D, DI)),
            whole(w_tail.shape),
            whole((1, HEADS)),
            whole((1, HEADS)),
        ],
        out_specs=(row(seq, DI), row(padded, DI), row(padded, 2 * STATE), row(padded, 128)),
        scratch_shapes=[
            pltpu.VMEM((3 * HEADS, DI), BF16),
            pltpu.VMEM((CHUNK, DI), F32),
            pltpu.VMEM((padded // CHUNK, 128, 128), F32),
        ],
        compiler_params=pltpu.CompilerParams(vmem_limit_bytes=40 * MIB),
        cost_estimate=pl.CostEstimate(
            flops=2 * total * D * 2400,
            bytes_accessed=2 * total * (D + 2 * DI) + 2 * D * 2400,
            transcendentals=total * DI,
        ),
    )(tok, w_in, w_tail, bias, alog)


def spread_last(cum, spread):
    last = jnp.broadcast_to(jnp.exp(cum[CHUNK - 1 : CHUNK, :]), (16, HEADS))
    return mm(split3(last), spread)[:1]


def state_kernel(x_ref, small_ref, decay_ref, starts_ref, end_ref, spread):
    seq = x_ref.shape[0]

    @pl.when(pl.program_id(0) == 0)
    def _():
        spread[...] = head_spread()

    state = jnp.zeros((STATE, DI), F32)
    count = starts_ref.shape[0] // STATE
    for k in range(count):
        size = min(CHUNK, seq - k * CHUNK)
        starts_ref[pl.ds(k * STATE, STATE), :] = state.astype(BF16)
        decay = decay_ref[pl.ds(k * CHUNK, CHUNK), :]
        cum, step = decay[:, :HEADS], decay[:, HEADS : 2 * HEADS]
        tail = (jnp.exp(cum[CHUNK - 1 :, :] - cum) * step)[:size]
        tail_wide = mm(split3(tail)[:, : 2 * HEADS], spread[: 2 * HEADS, :])
        x = x_ref[pl.ds(k * CHUNK, size), :].astype(F32)
        weighted = (x * tail_wide).astype(BF16)
        inject = small_ref[pl.ds(k * CHUNK, size), :STATE]
        added = lax.dot_general(inject, weighted, (((0,), (0,)), ((), ())), preferred_element_type=F32)
        state = spread_last(cum, spread[...]) * state + added
    end_ref[...] = state.astype(BF16)


def space_states(x, small, decay, frames):
    total = x.shape[0]
    seq = total // frames
    padded = decay.shape[0] // frames
    count = padded // CHUNK
    row = lambda n, width: pl.BlockSpec((n, width), lambda i: (i, 0))
    return pl.pallas_call(
        state_kernel,
        out_shape=(
            jax.ShapeDtypeStruct((frames * count * STATE, DI), BF16),
            jax.ShapeDtypeStruct((frames * STATE, DI), BF16),
        ),
        grid=(frames,),
        in_specs=[row(seq, DI), row(padded, 2 * STATE), row(padded, 128)],
        out_specs=(row(count * STATE, DI), row(STATE, DI)),
        scratch_shapes=[pltpu.VMEM((3 * HEADS, DI), BF16)],
        compiler_params=pltpu.CompilerParams(vmem_limit_bytes=32 * MIB),
        cost_estimate=pl.CostEstimate(
            flops=2 * total * 128 * DI, bytes_accessed=4 * total * DI, transcendentals=0
        ),
    )(x, small, decay)


def local_kernel(x_ref, w_ref, skip_ref, out_ref):
    seq = x_ref.shape[0]
    for k in range(w_ref.shape[0] // CHUNK):
        size = min(CHUNK, seq - k * CHUNK)
        rows = pl.ds(k * CHUNK, size)
        for j in range(HEADS // 2):
            lanes = pl.ds(j * 128, 128)
            x_pair = x_ref[rows, lanes]
            padded = x_pair
            if size < CHUNK:
                padded = jnp.concatenate([x_pair, jnp.zeros((CHUNK - size, 128), BF16)], axis=0)
            local = mm(w_ref[rows, lanes], block_pair(padded))
            out_ref[rows, lanes] = local + skip_ref[:, lanes] * x_pair.astype(F32)


def space_local(x, weights, skip_wide, frames):
    total = x.shape[0]
    seq = total // frames
    padded = weights.shape[0] // frames
    row = lambda n, width: pl.BlockSpec((n, width), lambda i: (i, 0))
    return pl.pallas_call(
        local_kernel,
        out_shape=jax.ShapeDtypeStruct((total, DI), F32),
        grid=(frames,),
        in_specs=[
            row(seq, DI),
            row(padded, DI),
            pl.BlockSpec((1, DI), lambda i: (0, 0), pipeline_mode=pl.Buffered(1)),
        ],
        out_specs=row(seq, DI),
        compiler_params=pltpu.CompilerParams(vmem_limit_bytes=32 * MIB),
        cost_estimate=pl.CostEstimate(
            flops=2 * total * 128 * DI, bytes_accessed=8 * total * DI, transcendentals=0
        ),
    )(x, weights, skip_wide)


def finish_kernel(local_ref, z_ref, small_ref, decay_ref, starts_ref, from_ref, gain_ref, wo_ref, tok_ref, out_ref, spread, y_ref):
    seq = local_ref.shape[0]

    @pl.when(pl.program_id(0) == 0)
    def _():
        spread[...] = head_spread()

    offset = jnp.zeros((1, HEADS), F32)
    entering = from_ref[...].astype(F32)
    for k in range(decay_ref.shape[0] // CHUNK):
        size = min(CHUNK, seq - k * CHUNK)
        rows = pl.ds(k * CHUNK, size)
        cum = decay_ref[pl.ds(k * CHUNK, CHUNK), :HEADS]
        reach = mm(split3(jnp.broadcast_to(jnp.exp(offset), (16, HEADS))), spread[...])[:1]
        offset = offset + cum[CHUNK - 1 :, :]
        state = (starts_ref[pl.ds(k * STATE, STATE), :].astype(F32) + reach * entering).astype(BF16)
        carried = mm(small_ref[rows, STATE:], state)
        grown = mm(split3(jnp.exp(cum[:size])), spread[...])
        z = z_ref[rows, :].astype(F32)
        y = (local_ref[rows, :] + grown * carried) * (z * (1.0 / (1.0 + jnp.exp(-z))))
        scale = lax.rsqrt(jnp.mean(y * y, axis=1, keepdims=True) + 1e-5)
        y_ref[rows, :] = (y * scale * gain_ref[...]).astype(BF16)
    out_ref[...] = (mm(y_ref[...], wo_ref[...]) + tok_ref[...].astype(F32)).astype(BF16)


def finish(local, z, small, decay, starts, entering, gain, w_out, tok, frames):
    total = local.shape[0]
    seq = total // frames
    padded = decay.shape[0] // frames
    count = padded // CHUNK
    whole = lambda shape: pl.BlockSpec(shape, lambda i: (0, 0), pipeline_mode=pl.Buffered(1))
    row = lambda n, width: pl.BlockSpec((n, width), lambda i: (i, 0))
    return pl.pallas_call(
        finish_kernel,
        out_shape=jax.ShapeDtypeStruct((total, D), BF16),
        grid=(frames,),
        in_specs=[
            row(seq, DI),
            row(seq, DI),
            row(padded, 2 * STATE),
            row(padded, 128),
            row(count * STATE, DI),
            row(STATE, DI),
            whole((1, DI)),
            whole((DI, D)),
            row(seq, D),
        ],
        out_specs=row(seq, D),
        scratch_shapes=[pltpu.VMEM((3 * HEADS, DI), BF16), pltpu.VMEM((seq, DI), BF16)],
        compiler_params=pltpu.CompilerParams(vmem_limit_bytes=48 * MIB),
        cost_estimate=pl.CostEstimate(
            flops=2 * total * (D + 64) * DI, bytes_accessed=8 * total * DI, transcendentals=total * DI
        ),
    )(local, z, small, decay, starts, entering, gain, w_out, tok)


def space_exchange(end, totals):
    n = lax.axis_size("space")
    frames = totals.shape[0]
    part = end.shape[0] // n
    per_frame = STATE // part
    growth = jnp.exp(lax.all_gather(totals, "space"))
    mine = lax.axis_index("space") // per_frame
    growth = lax.dynamic_index_in_dim(growth, mine, axis=1, keepdims=False)
    growth = jnp.repeat(growth, HEAD_DIM, axis=1)[:, None, :]
    got = lax.all_to_all(end.reshape(n, part, DI), "space", 0, 0, tiled=True)
    running = jnp.zeros((part, DI), F32)
    starts = []
    for device in range(n):
        starts.append(running.astype(BF16))
        running = growth[device] * running + got[device].astype(F32)
    back = lax.all_to_all(jnp.stack(starts), "space", 0, 0, tiled=True)
    return back.reshape(frames * STATE, DI)


def body(
    tokens,
    w_in,
    w_out,
    a_log_time,
    a_log_space,
    dt_bias_time,
    dt_bias_space,
    skip_time,
    skip_space,
    norm_gain,
):
    frames = tokens.shape[0]
    n_tm = lax.axis_size("tm")
    flat = tokens.reshape(-1, D)
    seq = flat.shape[0] // frames
    items = seq // n_tm
    w_tail = w_in[:, 2 * DI :]
    one = lambda v: v.reshape(1, -1)
    wide = lambda v: jnp.repeat(v, HEAD_DIM).reshape(1, DI)

    got = lax.all_to_all(tokens.reshape(frames, n_tm, items, D), "tm", 1, 0, tiled=True)
    time_tok = jnp.swapaxes(got[:, 0], 0, 1).reshape(-1, D)
    gate, weights, small, decay = home_part(
        flat, w_in, w_tail, one(dt_bias_space), one(a_log_space), frames
    )
    time_out = time_scan(time_tok, w_in, w_tail, one(dt_bias_time), one(a_log_time), wide(skip_time), 5)
    returned = jnp.swapaxes(time_out.reshape(items, n_tm * frames, DI), 0, 1)[:, None]
    time_out = lax.all_to_all(returned, "tm", 0, 1, tiled=True).reshape(-1, DI)

    totals = decay.reshape(frames, -1, CHUNK, 128)[:, :, CHUNK - 1, :HEADS].sum(axis=1)
    starts, end = space_states(time_out, small, decay, frames)
    entering = space_exchange(end, totals)
    local = space_local(time_out, weights, wide(skip_space), frames)
    out = finish(local, gate, small, decay, starts, entering, one(norm_gain), w_out, flat, frames)
    return out.reshape(tokens.shape)


def solution(mesh):
    placed = (P("tm", "space", None, None), P(), P(), P(), P(), P(), P(), P(), P(), P())
    return jax.shard_map(
        body, mesh=mesh, in_specs=placed, out_specs=P("tm", "space", None, None), check_vma=False
    )
```

```python
import functools

import jax
import jax.numpy as jnp
from jax import lax
from jax.experimental import pallas as pl
from jax.experimental.pallas import tpu as pltpu
from jax.sharding import PartitionSpec as P

D = 1024
HEADS = 32
HEAD_DIM = 64
STATE = 64
DI = 2048
CHUNK = 64
F32 = jnp.float32
BF16 = jnp.bfloat16
MIB = 1 << 20


def mm(a, b):
    return jnp.dot(a, b, preferred_element_type=F32)


def softplus(v):
    return jnp.maximum(v, 0.0) + jnp.log1p(jnp.exp(-jnp.abs(v)))


def split3(v):
    hi = v.astype(BF16)
    rest = v - hi.astype(F32)
    mid = rest.astype(BF16)
    low = (rest - mid.astype(F32)).astype(BF16)
    return jnp.concatenate([hi, mid, low], axis=1)


def head_spread():
    row = lax.broadcasted_iota(jnp.int32, (3 * HEADS, DI), 0) % HEADS
    col = lax.broadcasted_iota(jnp.int32, (3 * HEADS, DI), 1) // HEAD_DIM
    return (row == col).astype(BF16)


def causal_ones():
    row = lax.broadcasted_iota(jnp.int32, (CHUNK, CHUNK), 0)
    col = lax.broadcasted_iota(jnp.int32, (CHUNK, CHUNK), 1)
    return row >= col


def chunk_cumsum(log_decay):
    tri = causal_ones().astype(F32).astype(BF16)
    wide = mm(tri, split3(log_decay))
    return wide[:, :HEADS] + wide[:, HEADS : 2 * HEADS] + wide[:, 2 * HEADS :]


def row_forms(cum, step):
    pair = jnp.concatenate([cum, step, jnp.zeros((CHUNK, 2 * HEADS), F32)], axis=1)
    return jnp.concatenate([pair, pair], axis=0).T


def pair_rows(turned_ref, base, j, lane_low):
    even = turned_ref[pl.ds(base + 2 * j, 1), :]
    odd = turned_ref[pl.ds(base + 2 * j + 1, 1), :]
    return jnp.where(lane_low, even, odd)


def decay_weights(cum_wide, turned_ref, scores2, j, lane_low):
    cum_row = pair_rows(turned_ref, 0, j, lane_low)
    step_row = pair_rows(turned_ref, HEADS, j, lane_low)
    span = jnp.exp(jnp.minimum(cum_wide - cum_row, 0.0))
    return (span * (scores2 * step_row)).astype(BF16)


def masked_scores(readout, inject):
    scores = lax.dot_general(readout, inject, (((1,), (1,)), ((), ())), preferred_element_type=F32)
    scores = jnp.where(causal_ones(), scores, 0.0)
    return jnp.concatenate([scores, scores], axis=1)


def block_pair(x_pair):
    low = lax.broadcasted_iota(jnp.int32, x_pair.shape, 1) < HEAD_DIM
    zero = jnp.zeros_like(x_pair)
    return jnp.concatenate([jnp.where(low, x_pair, zero), jnp.where(low, zero, x_pair)], axis=0)


def time_kernel(tok_ref, wx_ref, wt_ref, bias_ref, alog_ref, skip_ref, out_ref, spread, x_ref, small_ref, cum_ref, turned):
    items = tok_ref.shape[0] // CHUNK

    @pl.when(pl.program_id(0) == 0)
    def _():
        spread[...] = head_spread()

    tok = tok_ref[...]
    x_ref[...] = mm(tok, wx_ref[...]).astype(BF16)
    small_ref[...] = mm(tok, wt_ref[...]).astype(BF16)
    lane_low = lax.broadcasted_iota(jnp.int32, (1, 2 * CHUNK), 1) < CHUNK
    rate = -jnp.exp(alog_ref[...])

    def item(index, carry):
        rows = pl.ds(pl.multiple_of(index * CHUNK, CHUNK), CHUNK)
        small = small_ref[rows, :]
        scores2 = masked_scores(small[:, STATE : 2 * STATE], small[:, :STATE])
        step = softplus(small[:, 4 * STATE : 4 * STATE + HEADS].astype(F32) + bias_ref[...])
        cum = chunk_cumsum(rate * step)
        turned[...] = row_forms(cum, step)
        cum_ref[...] = mm(split3(cum), spread[...])
        for j in range(HEADS // 2):
            lanes = pl.ds(j * 128, 128)
            weights = decay_weights(cum_ref[:, lanes], turned, scores2, j, lane_low)
            x_pair = x_ref[rows, lanes]
            local = mm(weights, block_pair(x_pair))
            out_ref[rows, lanes] = (local + skip_ref[:, lanes] * x_pair.astype(F32)).astype(BF16)
        return carry

    lax.fori_loop(0, items, item, 0)


def time_scan(tok, w_in, w_tail, bias, alog, skip_wide, per_step):
    rows = per_step * CHUNK
    total = tok.shape[0]
    whole = lambda shape: pl.BlockSpec(shape, lambda i: (0, 0), pipeline_mode=pl.Buffered(1))
    return pl.pallas_call(
        time_kernel,
        out_shape=jax.ShapeDtypeStruct((total, DI), BF16),
        grid=(total // rows,),
        in_specs=[
            pl.BlockSpec((rows, D), lambda i: (i, 0)),
            pl.BlockSpec((D, DI), lambda i: (0, 1), pipeline_mode=pl.Buffered(1)),
            whole(w_tail.shape),
            whole((1, HEADS)),
            whole((1, HEADS)),
            whole((1, DI)),
        ],
        out_specs=pl.BlockSpec((rows, DI), lambda i: (i, 0)),
        scratch_shapes=[
            pltpu.VMEM((3 * HEADS, DI), BF16),
            pltpu.VMEM((rows, DI), BF16),
            pltpu.VMEM((rows, w_tail.shape[1]), BF16),
            pltpu.VMEM((CHUNK, DI), F32),
            pltpu.VMEM((128, 128), F32),
        ],
        compiler_params=pltpu.CompilerParams(vmem_limit_bytes=40 * MIB),
        cost_estimate=pl.CostEstimate(
            flops=2 * total * D * 2400 + 2 * total * 128 * DI,
            bytes_accessed=2 * total * (D + DI) + 2 * D * 2400,
            transcendentals=total * DI,
        ),
    )(tok, w_in, w_tail, bias, alog, skip_wide)


def home_kernel(tok_ref, wz_ref, wt_ref, bias_ref, alog_ref, z_ref, w_ref, small_ref, decay_ref, spread, cum_ref, turned):
    seq = tok_ref.shape[0]

    @pl.when(pl.program_id(0) == 0)
    def _():
        spread[...] = head_spread()

    tok = tok_ref[...]
    z_ref[...] = mm(tok, wz_ref[...]).astype(BF16)
    tail = mm(tok, wt_ref[...])
    inject = tail[:, 2 * STATE : 3 * STATE].astype(BF16)
    readout = tail[:, 3 * STATE : 4 * STATE].astype(BF16)
    step = softplus(tail[:, 4 * STATE + HEADS : 4 * STATE + 2 * HEADS] + bias_ref[...])
    pad = w_ref.shape[0] - seq
    inject = jnp.concatenate([inject, jnp.zeros((pad, STATE), BF16)], axis=0)
    readout = jnp.concatenate([readout, jnp.zeros((pad, STATE), BF16)], axis=0)
    step = jnp.concatenate([step, jnp.zeros((pad, HEADS), F32)], axis=0)
    small_ref[...] = jnp.concatenate([inject, readout], axis=1)
    log_decay = -jnp.exp(alog_ref[...]) * step
    lane_low = lax.broadcasted_iota(jnp.int32, (1, 2 * CHUNK), 1) < CHUNK
    for k in range(w_ref.shape[0] // CHUNK):
        rows = pl.ds(k * CHUNK, CHUNK)
        part = slice(k * CHUNK, (k + 1) * CHUNK)
        cum = chunk_cumsum(log_decay[part])
        decay_ref[rows, :] = jnp.concatenate(
            [cum, step[part], jnp.zeros((CHUNK, 2 * HEADS), F32)], axis=1
        )
        turned[k] = row_forms(cum, step[part])
        cum_ref[...] = mm(split3(cum), spread[...])
        scores2 = masked_scores(readout[part], inject[part])
        for j in range(HEADS // 2):
            lanes = pl.ds(j * 128, 128)
            w_ref[rows, lanes] = decay_weights(cum_ref[:, lanes], turned.at[k], scores2, j, lane_low)


def home_part(tok, w_in, w_tail, bias, alog, frames):
    total = tok.shape[0]
    seq = total // frames
    padded = -(-seq // CHUNK) * CHUNK
    whole = lambda shape: pl.BlockSpec(shape, lambda i: (0, 0), pipeline_mode=pl.Buffered(1))
    row = lambda n, width: pl.BlockSpec((n, width), lambda i: (i, 0))
    return pl.pallas_call(
        home_kernel,
        out_shape=(
            jax.ShapeDtypeStruct((total, DI), BF16),
            jax.ShapeDtypeStruct((frames * padded, DI), BF16),
            jax.ShapeDtypeStruct((frames * padded, 2 * STATE), BF16),
            jax.ShapeDtypeStruct((frames * padded, 128), F32),
        ),
        grid=(frames,),
        in_specs=[
            row(seq, D),
            whole((D, DI)),
            whole(w_tail.shape),
            whole((1, HEADS)),
            whole((1, HEADS)),
        ],
        out_specs=(row(seq, DI), row(padded, DI), row(padded, 2 * STATE), row(padded, 128)),
        scratch_shapes=[
            pltpu.VMEM((3 * HEADS, DI), BF16),
            pltpu.VMEM((CHUNK, DI), F32),
            pltpu.VMEM((padded // CHUNK, 128, 128), F32),
        ],
        compiler_params=pltpu.CompilerParams(vmem_limit_bytes=40 * MIB),
        cost_estimate=pl.CostEstimate(
            flops=2 * total * D * 2400,
            bytes_accessed=2 * total * (D + 2 * DI) + 2 * D * 2400,
            transcendentals=total * DI,
        ),
    )(tok, w_in, w_tail, bias, alog)


def widen(values, spread):
    return mm(split3(values), spread[...])


def last_row(values):
    return jnp.broadcast_to(values[CHUNK - 1 :, :], (16, HEADS))


def back_kernel(
    n,
    x_hbm,
    w_hbm,
    z_hbm,
    tok_hbm,
    wo_hbm,
    small_ref,
    decay_ref,
    skip_ref,
    gain_ref,
    out_ref,
    x_v,
    w_v,
    z_v,
    tok_v,
    wo_v,
    starts,
    end,
    got,
    leaving,
    entering,
    tot_mine,
    tot_got,
    growth,
    running,
    local,
    y_v,
    spread,
    load_sem,
    send_sem,
    recv_sem,
    tot_send,
    tot_recv,
    back_send,
    back_recv,
):
    frames, seq = x_v.shape[0], x_v.shape[1]
    count = w_v.shape[1] // CHUNK
    halves = n // frames
    part = STATE // halves
    me = lax.axis_index("space")

    def load(kind, f):
        src, dst = ((x_hbm, x_v), (w_hbm, w_v), (z_hbm, z_v), (tok_hbm, tok_v))[kind]
        return pltpu.make_async_copy(src.at[f], dst.at[f], load_sem.at[kind, f])

    weight_load = pltpu.make_async_copy(wo_hbm, wo_v, load_sem.at[4, 0])
    for kind in range(4):
        for f in range(frames):
            load(kind, f).start()
    weight_load.start()

    def remote(src, dst, send, recv, device):
        return pltpu.make_async_remote_copy(
            src_ref=src,
            dst_ref=dst,
            send_sem=send,
            recv_sem=recv,
            device_id={"space": device},
            device_id_type=pl.DeviceIdType.MESH,
        )

    def state_copy(g, slot):
        return remote(end.at[g], got.at[slot], send_sem.at[g], recv_sem.at[slot], g)

    def tot_copy(g, slot):
        return remote(tot_mine.at[g // halves], tot_got.at[slot], tot_send.at[g], tot_recv.at[slot], g)

    def back_copy(g, slot):
        return remote(leaving.at[g], entering.at[slot], back_send.at[g], back_recv.at[slot], g)

    barrier = pltpu.get_barrier_semaphore()
    for step in range(1, n):
        pl.semaphore_signal(
            barrier,
            inc=1,
            device_id={"space": lax.rem(me + step, n)},
            device_id_type=pl.DeviceIdType.MESH,
        )
    spread[...] = head_spread()
    pl.semaphore_wait(barrier, n - 1)

    def states(f, carry):
        load(0, f).wait()
        state = jnp.zeros((STATE, DI), F32)
        total = jnp.zeros((16, HEADS), F32)
        for k in range(count):
            size = min(CHUNK, seq - k * CHUNK)
            starts[f, pl.ds(k * STATE, STATE), :] = state.astype(BF16)
            decay = decay_ref[f, pl.ds(k * CHUNK, CHUNK), :]
            cum, step = decay[:, :HEADS], decay[:, HEADS : 2 * HEADS]
            tail = (jnp.exp(cum[CHUNK - 1 :, :] - cum) * step)[:size]
            weighted = (x_v[f, pl.ds(k * CHUNK, size), :].astype(F32) * widen(tail, spread)).astype(BF16)
            inject = small_ref[f, pl.ds(k * CHUNK, size), :STATE]
            added = lax.dot_general(
                inject, weighted, (((0,), (0,)), ((), ())), preferred_element_type=F32
            )
            state = widen(last_row(jnp.exp(cum)), spread)[:1] * state + added
            total = total + last_row(cum)
        tot_mine[f] = jnp.concatenate([total[:8], jnp.zeros((8, 128 - HEADS), F32)], axis=1)
        for half in range(halves):
            g = halves * f + half
            end[g] = state[half * part : (half + 1) * part].astype(BF16)

            @pl.when(g != me)
            def _():
                state_copy(g, me).start()
                tot_copy(g, me).start()

            @pl.when(g == me)
            def _():
                got[me] = end[me]
                tot_got[me] = tot_mine[f]

        return carry

    lax.fori_loop(0, frames, states, 0)

    def locals_of(f, carry):
        load(1, f).wait()
        for k in range(count):
            size = min(CHUNK, seq - k * CHUNK)
            rows = pl.ds(k * CHUNK, size)
            for j in range(HEADS // 2):
                lanes = pl.ds(j * 128, 128)
                x_pair = x_v[f, rows, lanes]
                padded = x_pair
                if size < CHUNK:
                    padded = jnp.concatenate([x_pair, jnp.zeros((CHUNK - size, 128), BF16)], axis=0)
                mixed = mm(w_v[f, rows, lanes], block_pair(padded))
                local[f, rows, lanes] = mixed + skip_ref[:, lanes] * x_pair.astype(F32)
        return carry

    lax.fori_loop(0, frames, locals_of, 0)

    def wait_total(s, carry):
        @pl.when(s != me)
        def _():
            tot_copy(s, s).wait_recv()

        return carry

    lax.fori_loop(0, n, wait_total, 0)
    totals = jnp.concatenate([tot_got[s] for s in range(n)], axis=0)[:, :HEADS]
    growth[...] = widen(jnp.exp(totals), spread)
    running[...] = jnp.zeros_like(running)

    def relay(s, carry):
        @pl.when(s != me)
        def _():
            leaving[s] = running[...].astype(BF16)
            back_copy(s, me).start()
            state_copy(s, s).wait_recv()

        @pl.when(s == me)
        def _():
            entering[me] = running[...].astype(BF16)

        rate = growth[pl.ds(pl.multiple_of(s * 8, 8), 1), :]
        running[...] = rate * running[...] + got[s].astype(F32)
        return carry

    lax.fori_loop(0, n, relay, 0)
    weight_load.wait()

    def finish(f, carry):
        load(2, f).wait()
        load(3, f).wait()
        for half in range(halves):
            g = halves * f + half

            @pl.when(g != me)
            def _():
                back_copy(g, g).wait_recv()

        arrived = jnp.concatenate([entering[halves * f + half] for half in range(halves)], axis=0)
        arrived = arrived.astype(F32)
        offset = jnp.zeros((16, HEADS), F32)
        for k in range(count):
            size = min(CHUNK, seq - k * CHUNK)
            rows = pl.ds(k * CHUNK, size)
            cum = decay_ref[f, pl.ds(k * CHUNK, CHUNK), :HEADS]
            reach = widen(jnp.exp(offset), spread)[:1]
            offset = offset + last_row(cum)
            state = starts[f, pl.ds(k * STATE, STATE), :].astype(F32) + reach * arrived
            carried = mm(small_ref[f, rows, STATE:], state.astype(BF16))
            z = z_v[f, rows, :].astype(F32)
            y = local[f, rows, :] + widen(jnp.exp(cum[:size]), spread) * carried
            y = y * (z * (1.0 / (1.0 + jnp.exp(-z))))
            scale = lax.rsqrt(jnp.mean(y * y, axis=1, keepdims=True) + 1e-5)
            y_v[rows, :] = (y * scale * gain_ref[...]).astype(BF16)
        out_ref[f] = (mm(y_v[...], wo_v[...]) + tok_v[f].astype(F32)).astype(BF16)
        return carry

    lax.fori_loop(0, frames, finish, 0)

    def drain(g, carry):
        @pl.when(g != me)
        def _():
            state_copy(g, me).wait_send()
            tot_copy(g, me).wait_send()
            back_copy(g, me).wait_send()

        return carry

    lax.fori_loop(0, n, drain, 0)


def back_part(x, weights, z, tok, w_out, small, decay, skip_wide, gain):
    n = lax.axis_size("space")
    frames, seq = x.shape[0], x.shape[1]
    padded = weights.shape[1]
    count = padded // CHUNK
    part = frames * STATE // n
    anywhere = pl.BlockSpec(memory_space=pl.ANY)
    in_vmem = pl.BlockSpec(memory_space=pltpu.VMEM)
    dma = pltpu.SemaphoreType.DMA
    return pl.pallas_call(
        functools.partial(back_kernel, n),
        out_shape=jax.ShapeDtypeStruct((frames, seq, D), BF16),
        in_specs=[anywhere] * 5 + [in_vmem] * 4,
        out_specs=in_vmem,
        scratch_shapes=[
            pltpu.VMEM((frames, seq, DI), BF16),
            pltpu.VMEM((frames, padded, DI), BF16),
            pltpu.VMEM((frames, seq, DI), BF16),
            pltpu.VMEM((frames, seq, D), BF16),
            pltpu.VMEM((DI, D), BF16),
            pltpu.VMEM((frames, count * STATE, DI), BF16),
            pltpu.VMEM((n, part, DI), BF16),
            pltpu.VMEM((n, part, DI), BF16),
            pltpu.VMEM((n, part, DI), BF16),
            pltpu.VMEM((n, part, DI), BF16),
            pltpu.VMEM((frames, 8, 128), F32),
            pltpu.VMEM((n, 8, 128), F32),
            pltpu.VMEM((n * 8, DI), F32),
            pltpu.VMEM((part, DI), F32),
            pltpu.VMEM((frames, seq, DI), F32),
            pltpu.VMEM((seq, DI), BF16),
            pltpu.VMEM((3 * HEADS, DI), BF16),
            dma((5, frames)),
            dma((n,)),
            dma((n,)),
            dma((n,)),
            dma((n,)),
            dma((n,)),
            dma((n,)),
        ],
        compiler_params=pltpu.CompilerParams(
            collective_id=0, has_side_effects=True, vmem_limit_bytes=56 * MIB
        ),
    )(x, weights, z, tok, w_out, small, decay, skip_wide, gain)


def body(
    tokens,
    w_in,
    w_out,
    a_log_time,
    a_log_space,
    dt_bias_time,
    dt_bias_space,
    skip_time,
    skip_space,
    norm_gain,
):
    frames = tokens.shape[0]
    n_tm = lax.axis_size("tm")
    flat = tokens.reshape(-1, D)
    seq = flat.shape[0] // frames
    items = seq // n_tm
    w_tail = w_in[:, 2 * DI :]
    one = lambda v: v.reshape(1, -1)
    wide = lambda v: jnp.repeat(v, HEAD_DIM).reshape(1, DI)

    got = lax.all_to_all(tokens.reshape(frames, n_tm, items, D), "tm", 1, 0, tiled=True)
    time_tok = jnp.swapaxes(got[:, 0], 0, 1).reshape(-1, D)
    gate, weights, small, decay = home_part(
        flat, w_in, w_tail, one(dt_bias_space), one(a_log_space), frames
    )
    time_out = time_scan(time_tok, w_in, w_tail, one(dt_bias_time), one(a_log_time), wide(skip_time), 5)
    returned = jnp.swapaxes(time_out.reshape(items, n_tm * frames, DI), 0, 1)[:, None]
    time_out = lax.all_to_all(returned, "tm", 0, 1, tiled=True).reshape(-1, DI)

    framed = lambda v: v.reshape(frames, -1, v.shape[-1])
    out = back_part(
        framed(time_out),
        framed(weights),
        framed(gate),
        framed(flat),
        w_out,
        framed(small),
        framed(decay),
        wide(skip_space),
        one(norm_gain),
    )
    return out.reshape(tokens.shape)


def solution(mesh):
    placed = (P("tm", "space", None, None), P(), P(), P(), P(), P(), P(), P(), P(), P())
    return jax.shard_map(
        body, mesh=mesh, in_specs=placed, out_specs=P("tm", "space", None, None), check_vma=False
    )
```

```python
import functools

import jax
import jax.numpy as jnp
from jax import lax
from jax.experimental import pallas as pl
from jax.experimental.pallas import tpu as pltpu
from jax.sharding import PartitionSpec as P

D = 1024
HEADS = 32
HEAD_DIM = 64
STATE = 64
DI = 2048
CHUNK = 64
F32 = jnp.float32
BF16 = jnp.bfloat16
MIB = 1 << 20


def mm(a, b):
    return jnp.dot(a, b, preferred_element_type=F32)


def softplus(v):
    return jnp.maximum(v, 0.0) + jnp.log1p(jnp.exp(-jnp.abs(v)))


def split3(v):
    hi = v.astype(BF16)
    rest = v - hi.astype(F32)
    mid = rest.astype(BF16)
    low = (rest - mid.astype(F32)).astype(BF16)
    return jnp.concatenate([hi, mid, low], axis=1)


def head_spread():
    row = lax.broadcasted_iota(jnp.int32, (3 * HEADS, DI), 0) % HEADS
    col = lax.broadcasted_iota(jnp.int32, (3 * HEADS, DI), 1) // HEAD_DIM
    return (row == col).astype(BF16)


def causal_ones():
    row = lax.broadcasted_iota(jnp.int32, (CHUNK, CHUNK), 0)
    col = lax.broadcasted_iota(jnp.int32, (CHUNK, CHUNK), 1)
    return row >= col


def chunk_cumsum(log_decay):
    tri = causal_ones().astype(F32).astype(BF16)
    wide = mm(tri, split3(log_decay))
    return wide[:, :HEADS] + wide[:, HEADS : 2 * HEADS] + wide[:, 2 * HEADS :]


def row_forms(cum, step):
    pair = jnp.concatenate([cum, step, jnp.zeros((CHUNK, 2 * HEADS), F32)], axis=1)
    return jnp.concatenate([pair, pair], axis=0).T


def pair_rows(turned_ref, base, j, lane_low):
    even = turned_ref[pl.ds(base + 2 * j, 1), :]
    odd = turned_ref[pl.ds(base + 2 * j + 1, 1), :]
    return jnp.where(lane_low, even, odd)


def decay_weights(cum_wide, turned_ref, scores2, j, lane_low):
    cum_row = pair_rows(turned_ref, 0, j, lane_low)
    step_row = pair_rows(turned_ref, HEADS, j, lane_low)
    span = jnp.exp(jnp.minimum(cum_wide - cum_row, 0.0))
    return (span * (scores2 * step_row)).astype(BF16)


def masked_scores(readout, inject):
    scores = lax.dot_general(readout, inject, (((1,), (1,)), ((), ())), preferred_element_type=F32)
    scores = jnp.where(causal_ones(), scores, 0.0)
    return jnp.concatenate([scores, scores], axis=1)


def block_pair(x_pair):
    low = lax.broadcasted_iota(jnp.int32, x_pair.shape, 1) < HEAD_DIM
    zero = jnp.zeros_like(x_pair)
    return jnp.concatenate([jnp.where(low, x_pair, zero), jnp.where(low, zero, x_pair)], axis=0)


ITEMS = 16
GROUP = 256
PAIRS = GROUP // 128
TOGETHER = 4
LAG = 1


def nt(a, b):
    return lax.dot_general(a, b, (((1,), (1,)), ((), ())), preferred_element_type=F32)


def tn(a, b):
    return lax.dot_general(a, b, (((0,), (0,)), ((), ())), preferred_element_type=F32)


def rounded(v):
    return v.astype(BF16).astype(F32)


def widen(values, spread):
    return mm(split3(values), spread[...])


def last_row(values):
    return jnp.broadcast_to(values[CHUNK - 1 :, :], (8, HEADS))


def block_kernel(
    n,
    n_space,
    tok_hbm,
    w_hbm,
    wo_hbm,
    bias_t_ref,
    alog_t_ref,
    skip_t_ref,
    bias_s_ref,
    alog_s_ref,
    skip_s_ref,
    gain_ref,
    out_ref,
    tok_v,
    tok_got,
    wz,
    wx,
    wt,
    z_v,
    w_v,
    x_group,
    cum_group,
    out_group,
    leaving,
    small_t,
    turned_t,
    turned_s,
    scores_t,
    cum3,
    cum_s,
    spread,
    skips,
    small_s,
    tail_s,
    grown_s,
    rate_s,
    reach_s,
    x_home,
    tot_mine,
    tot_got,
    growth,
    starts,
    end,
    got,
    going,
    entering,
    y_v,
    square,
    acc,
    load_sem,
    tok_send,
    tok_recv,
    ret_send,
    ret_recv,
    tot_send,
    tot_recv,
    st_send,
    st_recv,
    back_send,
    back_recv,
):
    frames, seq = tok_v.shape[0], tok_v.shape[1]
    padded = w_v.shape[1]
    count = padded // CHUNK
    holders = seq // ITEMS
    total = n * frames
    groups = DI // GROUP
    halves = n_space // frames
    part = STATE // halves
    me = lax.axis_index("tm")
    here = lax.axis_index("space")

    tok_load = pltpu.make_async_copy(tok_hbm, tok_v, load_sem.at[0])
    wz_load = pltpu.make_async_copy(w_hbm.at[pl.ds(0, DI)], wz, load_sem.at[1])
    wt_load = pltpu.make_async_copy(w_hbm.at[pl.ds(2 * DI, wt.shape[0])], wt, load_sem.at[2])
    wx_load = pltpu.make_async_copy(w_hbm.at[pl.ds(DI, DI)], wx, load_sem.at[3])
    wo_load = pltpu.make_async_copy(wo_hbm, wz, load_sem.at[4])
    tok_load.start()
    wt_load.start()
    wz_load.start()
    wx_load.start()

    def remote(src, dst, send, recv, axis, device):
        return pltpu.make_async_remote_copy(
            src_ref=src,
            dst_ref=dst,
            send_sem=send,
            recv_sem=recv,
            device_id={axis: device},
            device_id_type=pl.DeviceIdType.MESH,
        )

    def positions(d):
        return pl.ds(pl.multiple_of(d * ITEMS, ITEMS), ITEMS)

    def frame_rows(d):
        return pl.ds(d * frames, frames)

    def channels(g):
        return pl.ds(pl.multiple_of(g * GROUP, GROUP), GROUP)

    def pair_lanes(j):
        return pl.ds(pl.multiple_of(j * 128, 128), 128)

    def tok_copy(d, source):
        return remote(
            tok_hbm.at[:, positions(d), :],
            tok_got.at[frame_rows(source)],
            tok_send,
            tok_recv,
            "tm",
            d,
        )

    def ret_copy(d, source, g):
        return remote(
            leaving.at[g, frame_rows(d)],
            x_home.at[:, positions(source), channels(g)],
            ret_send,
            ret_recv.at[g],
            "tm",
            d,
        )

    def own_copy(g):
        return pltpu.make_async_copy(
            leaving.at[g, frame_rows(me)], x_home.at[:, positions(me), channels(g)], ret_recv.at[g]
        )

    own_tok = pltpu.make_async_copy(
        tok_hbm.at[:, positions(lax.rem(me, holders)), :], tok_got.at[frame_rows(me)], tok_recv
    )

    def tot_copy(s, slot):
        return remote(
            tot_mine.at[s // halves], tot_got.at[slot], tot_send, tot_recv, "space", s
        )

    def state_copy(s, slot, g):
        return remote(
            end.at[g, s], got.at[g, slot], st_send, st_recv.at[g], "space", s
        )

    def back_copy(s, slot, g):
        return remote(
            going.at[g, s], entering.at[g, slot], back_send, back_recv.at[g], "space", s
        )

    def wait_bytes(ref, sem):
        pltpu.make_async_copy(ref, ref, sem).wait()

    others = pl.ds(0, n_space - 1)
    barrier = pltpu.get_barrier_semaphore()
    for step in range(1, n):
        pl.semaphore_signal(
            barrier,
            inc=1,
            device_id={"tm": lax.rem(me + step, n)},
            device_id_type=pl.DeviceIdType.MESH,
        )
    for step in range(1, n_space):
        pl.semaphore_signal(
            barrier,
            inc=1,
            device_id={"space": lax.rem(here + step, n_space)},
            device_id_type=pl.DeviceIdType.MESH,
        )
    pl.semaphore_wait(barrier, n + n_space - 2)

    def send_tokens(step, carry):
        d = lax.rem(me + step, n)

        @pl.when(d < holders)
        def _():
            tok_copy(d, me).start()

        return carry

    lax.fori_loop(1, n, send_tokens, 0)

    @pl.when(me < holders)
    def _():
        own_tok.start()

    spread[...] = head_spread()
    skips[...] = widen(
        jnp.concatenate(
            [
                jnp.broadcast_to(skip_t_ref[...], (8, HEADS)),
                jnp.broadcast_to(skip_s_ref[...], (8, HEADS)),
            ],
            axis=0,
        ),
        spread,
    )
    square[...] = jnp.zeros_like(square)
    acc[...] = jnp.zeros_like(acc)
    lane_low = lax.broadcasted_iota(jnp.int32, (1, 2 * CHUNK), 1) < CHUNK
    tok_load.wait()
    wt_load.wait()
    wz_load.wait()

    def home(f, carry):
        tok = tok_v[f]
        z_v[f] = nt(tok, wz[...]).astype(BF16)
        tail = nt(tok, wt[...])
        inject = tail[:, 2 * STATE : 3 * STATE].astype(BF16)
        readout = tail[:, 3 * STATE : 4 * STATE].astype(BF16)
        step = softplus(tail[:, 4 * STATE + HEADS : 4 * STATE + 2 * HEADS] + bias_s_ref[...])
        pad = padded - seq
        inject = jnp.concatenate([inject, jnp.zeros((pad, STATE), BF16)], axis=0)
        readout = jnp.concatenate([readout, jnp.zeros((pad, STATE), BF16)], axis=0)
        step = jnp.concatenate([step, jnp.zeros((pad, HEADS), F32)], axis=0)
        small_s[f] = jnp.concatenate([inject, readout], axis=1)
        log_decay = -jnp.exp(alog_s_ref[...]) * step
        offset = jnp.zeros((8, HEADS), F32)
        for k in range(count):
            rows = pl.ds(k * CHUNK, CHUNK)
            part_k = slice(k * CHUNK, (k + 1) * CHUNK)
            cum = chunk_cumsum(log_decay[part_k])
            tail_k = jnp.exp(cum[CHUNK - 1 :, :] - cum) * step[part_k]
            tail_s[f, rows, :] = split3(tail_k)[:, : 2 * HEADS]
            grown_s[f, rows, :] = split3(jnp.exp(cum))
            both = widen(jnp.concatenate([jnp.exp(last_row(cum)), jnp.exp(offset)], axis=0), spread)
            rate_s[f, pl.ds(8 * k, 8), :] = both[:8]
            reach_s[f, pl.ds(8 * k, 8), :] = both[8:]
            offset = offset + last_row(cum)
            turned_s[k] = row_forms(cum, step[part_k])
            cum_s[...] = mm(split3(cum), spread[...])
            scores2 = masked_scores(readout[part_k], inject[part_k])
            for j in range(HEADS // 2):
                lanes = pl.ds(j * 128, 128)
                w_v[f, rows, lanes] = decay_weights(cum_s[:, lanes], turned_s.at[k], scores2, j, lane_low)
        tot_mine[f] = jnp.concatenate([offset, jnp.zeros((8, 128 - HEADS), F32)], axis=1)
        for half in range(halves):
            s = halves * f + half

            @pl.when(s != here)
            def _():
                tot_copy(s, here).start()

            @pl.when(s == here)
            def _():
                tot_got[here] = tot_mine[f]

        return carry

    lax.fori_loop(0, frames, home, 0)
    wo_load.start()
    wx_load.wait()

    @pl.when(me < holders)
    def _():
        wait_bytes(tok_got, tok_recv)
        tail = rounded(nt(tok_got[...].reshape(total * ITEMS, D), wt[...]))
        small_t[0] = tail[:, : 2 * STATE]
        small_t[1] = jnp.concatenate(
            [tail[:, 4 * STATE :], jnp.zeros((total * ITEMS, 128 - 2 * HEADS), F32)], axis=1
        )
        rate = -jnp.exp(alog_t_ref[...])

        def prepare(q, carry):
            several = [q * TOGETHER + u for u in range(TOGETHER)]
            rows = [pl.ds(p, CHUNK, stride=ITEMS) for p in several]
            pairs = [small_t[0, r, :].astype(BF16) for r in rows]
            steps = [softplus(small_t[1, r, :][:, :HEADS] + bias_t_ref[...]) for r in rows]
            scores = [masked_scores(pair[:, STATE:], pair[:, :STATE]) for pair in pairs]
            cums = [chunk_cumsum(rate * step) for step in steps]
            forms = [row_forms(cum, step) for cum, step in zip(cums, steps)]
            for u, p in enumerate(several):
                scores_t[p] = scores[u]
                turned_t[p] = forms[u]
                cum3[p] = split3(cums[u])
            return carry

        lax.fori_loop(0, ITEMS // TOGETHER, prepare, 0)

    wait_bytes(tot_got.at[others], tot_recv)
    totals = jnp.concatenate([tot_got[s] for s in range(n_space)], axis=0)[:, :HEADS]
    growth[...] = widen(jnp.exp(totals), spread)
    wo_load.wait()

    def scan_group(g):
        x = rounded(nt(tok_got[...].reshape(total * ITEMS, D), wx[channels(g), :]))
        cum = mm(cum3[...].reshape(ITEMS * CHUNK, 3 * HEADS), spread[:, channels(g)])
        for jj in range(PAIRS):
            x_group[jj] = x[:, jj * 128 : (jj + 1) * 128]
            cum_group[jj] = cum[:, jj * 128 : (jj + 1) * 128]

        def item(q, inner):
            work = [(q * TOGETHER + u, jj) for u in range(TOGETHER) for jj in range(PAIRS)]
            weights = [
                decay_weights(
                    cum_group[jj, pl.ds(pl.multiple_of(p * CHUNK, CHUNK), CHUNK), :],
                    turned_t.at[p],
                    scores_t[p],
                    g * PAIRS + jj,
                    lane_low,
                )
                for p, jj in work
            ]
            inputs = [x_group[jj, pl.ds(p, CHUNK, stride=ITEMS), :] for p, jj in work]
            mixed = [mm(w, block_pair(x.astype(BF16))) for w, x in zip(weights, inputs)]
            for u, (p, jj) in enumerate(work):
                skip = skips[pl.ds(0, 1), pair_lanes(g * PAIRS + jj)]
                out_group[jj, pl.ds(p, CHUNK, stride=ITEMS), :] = mixed[u] + skip * inputs[u]
            return inner

        lax.fori_loop(0, ITEMS // TOGETHER, item, 0)
        for jj in range(PAIRS):
            leaving[g, :, :, pl.ds(jj * 128, 128)] = (
                out_group[jj].astype(BF16).reshape(total, ITEMS, 128)
            )

        def send(step, inner):
            ret_copy(lax.rem(me + step, n), me, g).start()
            return inner

        lax.fori_loop(1, n, send, 0)
        own_copy(g).start()

    def states(g):
        wait_bytes(x_home.at[:, :, channels(g)], ret_recv.at[g])
        pieces = [(f, k, min(CHUNK, seq - k * CHUNK)) for f in range(frames) for k in range(count)]
        added = []
        for f, k, size in pieces:
            rows = pl.ds(k * CHUNK, size)
            tail_wide = mm(tail_s[f, rows, :], spread[: 2 * HEADS, channels(g)])
            weighted = (x_home[f, rows, channels(g)].astype(F32) * tail_wide).astype(BF16)
            added.append(tn(small_s[f, rows, :STATE], weighted))
        for f in range(frames):
            state = jnp.zeros((STATE, GROUP), F32)
            for k in range(count):
                starts[f, pl.ds(k * STATE, STATE), channels(g)] = state.astype(BF16)
                state = rate_s[f, pl.ds(8 * k, 1), channels(g)] * state + added[f * count + k]
            for half in range(halves):
                end[g, halves * f + half] = state[half * part : (half + 1) * part].astype(BF16)

        def send_state(step, carry):
            state_copy(lax.rem(here + step, n_space), here, g).start()
            return carry

        lax.fori_loop(1, n_space, send_state, 0)
        got[g, here] = end[g, here]

    def relay(g):
        wait_bytes(got.at[g, others], st_recv.at[g])
        running = jnp.zeros((part, GROUP), F32)
        for s in range(n_space):
            going[g, s] = running.astype(BF16)
            running = growth[pl.ds(8 * s, 1), channels(g)] * running + got[g, s].astype(F32)

        def send_back(step, carry):
            back_copy(lax.rem(here + step, n_space), here, g).start()
            return carry

        lax.fori_loop(1, n_space, send_back, 0)
        entering[g, here] = going[g, here]

    def finish(g):
        wait_bytes(entering.at[g, others], back_recv.at[g])

        def frame(f, carry):
            arrived = jnp.concatenate(
                [entering[g, halves * f + half] for half in range(halves)], axis=0
            ).astype(F32)
            sizes = [min(CHUNK, seq - k * CHUNK) for k in range(count)]
            carried, mixed = [], []
            for k, size in enumerate(sizes):
                rows = pl.ds(k * CHUNK, size)
                reach = reach_s[f, pl.ds(8 * k, 1), channels(g)]
                state = starts[f, pl.ds(k * STATE, STATE), channels(g)].astype(F32) + reach * arrived
                product = mm(small_s[f, rows, STATE:], state.astype(BF16))
                carried.append(product * mm(grown_s[f, rows, :], spread[:, channels(g)]))
                for jj in range(PAIRS):
                    lanes = pair_lanes(g * PAIRS + jj)
                    full = x_home[f, rows, lanes]
                    if size < CHUNK:
                        full = jnp.concatenate([full, jnp.zeros((CHUNK - size, 128), BF16)], axis=0)
                    mixed.append(mm(w_v[f, rows, lanes], block_pair(full)))
            for k, size in enumerate(sizes):
                rows = pl.ds(k * CHUNK, size)
                energy = square[f, rows, :]
                for jj in range(PAIRS):
                    lanes = pair_lanes(g * PAIRS + jj)
                    y = mixed[k * PAIRS + jj] + carried[k][:, jj * 128 : (jj + 1) * 128]
                    y = y + skips[pl.ds(8, 1), lanes] * x_home[f, rows, lanes].astype(F32)
                    z = z_v[f, rows, lanes].astype(F32)
                    y = y * (z * (1.0 / (1.0 + jnp.exp(-z))))
                    energy = energy + y * y
                    y_v[f, rows, pl.ds(jj * 128, 128)] = (y * gain_ref[:, lanes]).astype(BF16)
                square[f, rows, :] = energy
            return carry

        lax.fori_loop(0, frames, frame, 0)
        y_all = y_v[...].reshape(frames * seq, GROUP)
        acc[...] += mm(y_all, wz[channels(g), :])

    def advance(i, carry):
        @pl.when(jnp.logical_and(i < groups, me < holders))
        def _():
            scan_group(i)

        @pl.when(jnp.logical_and(i >= LAG, i < groups + LAG))
        def _():
            states(i - LAG)

        @pl.when(jnp.logical_and(i >= LAG + 1, i < groups + LAG + 1))
        def _():
            relay(i - LAG - 1)

        @pl.when(i >= LAG + 2)
        def _():
            finish(i - LAG - 2)

        return carry

    lax.fori_loop(0, groups + LAG + 2, advance, 0)

    def close(f, carry):
        mean = jnp.sum(square[f], axis=1, keepdims=True) * (1.0 / DI)
        scale = lax.rsqrt(mean + 1e-5)
        product = acc[pl.ds(pl.multiple_of(f * seq, 16), seq), :]
        out_ref[f] = (product * scale + tok_v[f].astype(F32)).astype(BF16)
        return carry

    lax.fori_loop(0, frames, close, 0)

    @pl.when(me < holders)
    def _():
        wait_bytes(tok_got.at[pl.ds(0, frames * (holders - 1))], tok_send)
        wait_bytes(leaving.at[:, pl.ds(0, frames * (n - 1))], ret_send)

    @pl.when(me >= holders)
    def _():
        wait_bytes(tok_got.at[pl.ds(0, frames * holders)], tok_send)

    wait_bytes(tot_got.at[others], tot_send)
    wait_bytes(end.at[:, others], st_send)
    wait_bytes(going.at[:, others], back_send)


def block(tok, w_turned, w_out, bias_t, alog_t, skip_t, bias_s, alog_s, skip_s, gain):
    n = lax.axis_size("tm")
    n_space = lax.axis_size("space")
    frames, seq = tok.shape[0], tok.shape[1]
    padded = -(-seq // CHUNK) * CHUNK
    count = padded // CHUNK
    total = n * frames
    groups = DI // GROUP
    part = frames * STATE // n_space
    tail = w_turned.shape[0] - 2 * DI
    anywhere = pl.BlockSpec(memory_space=pl.ANY)
    in_vmem = pl.BlockSpec(memory_space=pltpu.VMEM)
    dma = pltpu.SemaphoreType.DMA
    vmem = pltpu.VMEM
    return pl.pallas_call(
        functools.partial(block_kernel, n, n_space),
        out_shape=jax.ShapeDtypeStruct((frames, seq, D), BF16),
        in_specs=[anywhere] * 3 + [in_vmem] * 7,
        out_specs=in_vmem,
        scratch_shapes=[
            vmem((frames, seq, D), BF16),
            vmem((total, ITEMS, D), BF16),
            vmem((DI, D), BF16),
            vmem((DI, D), BF16),
            vmem((tail, D), BF16),
            vmem((frames, seq, DI), BF16),
            vmem((frames, padded, DI), BF16),
            vmem((PAIRS, total * ITEMS, 128), F32),
            vmem((PAIRS, total * ITEMS, 128), F32),
            vmem((PAIRS, total * ITEMS, 128), F32),
            vmem((groups, total, ITEMS, GROUP), BF16),
            vmem((2, total * ITEMS, 128), F32),
            vmem((ITEMS, 128, 128), F32),
            vmem((count, 128, 128), F32),
            vmem((ITEMS, CHUNK, 128), F32),
            vmem((ITEMS, CHUNK, 3 * HEADS), BF16),
            vmem((CHUNK, DI), F32),
            vmem((3 * HEADS, DI), BF16),
            vmem((16, DI), F32),
            vmem((frames, padded, 2 * STATE), BF16),
            vmem((frames, padded, 2 * HEADS), BF16),
            vmem((frames, padded, 3 * HEADS), BF16),
            vmem((frames, 8 * count, DI), F32),
            vmem((frames, 8 * count, DI), F32),
            vmem((frames, seq, DI), BF16),
            vmem((frames, 8, 128), F32),
            vmem((n_space, 8, 128), F32),
            vmem((n_space * 8, DI), F32),
            vmem((frames, count * STATE, DI), BF16),
            vmem((groups, n_space, part, GROUP), BF16),
            vmem((groups, n_space, part, GROUP), BF16),
            vmem((groups, n_space, part, GROUP), BF16),
            vmem((groups, n_space, part, GROUP), BF16),
            vmem((frames, seq, GROUP), BF16),
            vmem((frames, seq, 128), F32),
            vmem((frames * seq, D), F32),
            dma((5,)),
            dma(()),
            dma(()),
            dma(()),
            dma((groups,)),
            dma(()),
            dma(()),
            dma(()),
            dma((groups,)),
            dma(()),
            dma((groups,)),
        ],
        compiler_params=pltpu.CompilerParams(
            collective_id=0, has_side_effects=True, vmem_limit_bytes=60 * MIB
        ),
    )(tok, w_turned, w_out, bias_t, alog_t, skip_t, bias_s, alog_s, skip_s, gain)


def body(
    tokens,
    w_in,
    w_out,
    a_log_time,
    a_log_space,
    dt_bias_time,
    dt_bias_space,
    skip_time,
    skip_space,
    norm_gain,
):
    frames = tokens.shape[0]
    tok = tokens.reshape(frames, -1, D)
    one = lambda v: v.reshape(1, -1)
    out = block(
        tok,
        w_in.T,
        w_out,
        one(dt_bias_time),
        one(a_log_time),
        one(skip_time),
        one(dt_bias_space),
        one(a_log_space),
        one(skip_space),
        one(norm_gain),
    )
    return out.reshape(tokens.shape)


def solution(mesh):
    placed = (P("tm", "space", None, None), P(), P(), P(), P(), P(), P(), P(), P(), P())
    return jax.shard_map(
        body, mesh=mesh, in_specs=placed, out_specs=P("tm", "space", None, None), check_vma=False
    )
```

```python
import functools

import jax
import jax.numpy as jnp
from jax import lax
from jax.experimental import pallas as pl
from jax.experimental.pallas import tpu as pltpu
from jax.sharding import PartitionSpec as P

D = 1024
HEADS = 32
HEAD_DIM = 64
STATE = 64
DI = 2048
CHUNK = 64
F32 = jnp.float32
BF16 = jnp.bfloat16
MIB = 1 << 20


def mm(a, b):
    return jnp.dot(a, b, preferred_element_type=F32)


def softplus(v):
    return jnp.maximum(v, 0.0) + jnp.log1p(jnp.exp(-jnp.abs(v)))


def split3(v):
    hi = v.astype(BF16)
    rest = v - hi.astype(F32)
    mid = rest.astype(BF16)
    low = (rest - mid.astype(F32)).astype(BF16)
    return jnp.concatenate([hi, mid, low], axis=1)


def head_spread():
    row = lax.broadcasted_iota(jnp.int32, (3 * HEADS, DI), 0) % HEADS
    col = lax.broadcasted_iota(jnp.int32, (3 * HEADS, DI), 1) // HEAD_DIM
    return (row == col).astype(BF16)


def causal_ones():
    row = lax.broadcasted_iota(jnp.int32, (CHUNK, CHUNK), 0)
    col = lax.broadcasted_iota(jnp.int32, (CHUNK, CHUNK), 1)
    return row >= col


def chunk_cumsum(log_decay):
    tri = causal_ones().astype(F32).astype(BF16)
    wide = mm(tri, split3(log_decay))
    return wide[:, :HEADS] + wide[:, HEADS : 2 * HEADS] + wide[:, 2 * HEADS :]


def row_forms(cum, step):
    pair = jnp.concatenate([cum, step, jnp.zeros((CHUNK, 2 * HEADS), F32)], axis=1)
    return jnp.concatenate([pair, pair], axis=0).T


def pair_rows(turned_ref, base, j, lane_low):
    even = turned_ref[pl.ds(base + 2 * j, 1), :]
    odd = turned_ref[pl.ds(base + 2 * j + 1, 1), :]
    return jnp.where(lane_low, even, odd)


def decay_weights(cum_wide, turned_ref, scores2, j, lane_low):
    cum_row = pair_rows(turned_ref, 0, j, lane_low)
    step_row = pair_rows(turned_ref, HEADS, j, lane_low)
    span = jnp.exp(jnp.minimum(cum_wide - cum_row, 0.0))
    return (span * (scores2 * step_row)).astype(BF16)


def masked_scores(readout, inject):
    scores = lax.dot_general(readout, inject, (((1,), (1,)), ((), ())), preferred_element_type=F32)
    scores = jnp.where(causal_ones(), scores, 0.0)
    return jnp.concatenate([scores, scores], axis=1)


def block_pair(x_pair):
    low = lax.broadcasted_iota(jnp.int32, x_pair.shape, 1) < HEAD_DIM
    zero = jnp.zeros_like(x_pair)
    return jnp.concatenate([jnp.where(low, x_pair, zero), jnp.where(low, zero, x_pair)], axis=0)


ITEMS = 16
GROUP = 512
PAIRS = GROUP // 128
TOGETHER = 4
LAG = 2
HALF = 8
ROUNDS = ITEMS // HALF


def nt(a, b):
    return lax.dot_general(a, b, (((1,), (1,)), ((), ())), preferred_element_type=F32)


def tn(a, b):
    return lax.dot_general(a, b, (((0,), (0,)), ((), ())), preferred_element_type=F32)


def rounded(v):
    return v.astype(BF16).astype(F32)


def widen(values, spread):
    return mm(split3(values), spread[...])


def last_row(values):
    return jnp.broadcast_to(values[CHUNK - 1 :, :], (8, HEADS))


def block_kernel(
    n,
    n_space,
    tok_hbm,
    w_hbm,
    wo_hbm,
    bias_t_ref,
    alog_t_ref,
    skip_t_ref,
    bias_s_ref,
    alog_s_ref,
    skip_s_ref,
    gain_ref,
    out_ref,
    tok_v,
    tok_got,
    wz,
    wx,
    wt,
    z_v,
    w_v,
    x_group,
    cum_group,
    out_group,
    leaving,
    small_t,
    turned_t,
    turned_s,
    scores_t,
    cum3,
    cum_s,
    spread,
    skips,
    small_s,
    tail_s,
    grown_s,
    rate_s,
    reach_s,
    x_home,
    tot_mine,
    tot_got,
    growth,
    starts,
    end,
    got,
    going,
    entering,
    y_v,
    square,
    acc,
    load_sem,
    tok_send,
    tok_recv,
    ret_send,
    ret_recv,
    tot_send,
    tot_recv,
    st_send,
    st_recv,
    back_send,
    back_recv,
):
    frames, seq = tok_v.shape[0], tok_v.shape[1]
    padded = w_v.shape[1]
    count = padded // CHUNK
    holders = seq // ITEMS
    total = n * frames
    groups = DI // GROUP
    halves = n_space // frames
    part = STATE // halves
    me = lax.axis_index("tm")
    here = lax.axis_index("space")

    tok_load = pltpu.make_async_copy(tok_hbm, tok_v, load_sem.at[0])
    wz_load = pltpu.make_async_copy(w_hbm.at[pl.ds(0, DI)], wz, load_sem.at[1])
    wt_load = pltpu.make_async_copy(w_hbm.at[pl.ds(2 * DI, wt.shape[0])], wt, load_sem.at[2])
    wx_load = pltpu.make_async_copy(w_hbm.at[pl.ds(DI, DI)], wx, load_sem.at[3])
    wo_load = pltpu.make_async_copy(wo_hbm, wz, load_sem.at[4])
    tok_load.start()
    wt_load.start()
    wz_load.start()
    wx_load.start()

    def remote(src, dst, send, recv, axis, device):
        return pltpu.make_async_remote_copy(
            src_ref=src,
            dst_ref=dst,
            send_sem=send,
            recv_sem=recv,
            device_id={axis: device},
            device_id_type=pl.DeviceIdType.MESH,
        )

    def frame_rows(d):
        return pl.ds(d * frames, frames)

    def channels(g):
        return pl.ds(pl.multiple_of(g * GROUP, GROUP), GROUP)

    def pair_lanes(j):
        return pl.ds(pl.multiple_of(j * 128, 128), 128)

    def block_of(d, h):
        return pl.ds(pl.multiple_of(d * ITEMS + h * HALF, HALF), HALF)

    def tok_copy(d, source, h):
        return remote(
            tok_hbm.at[:, block_of(d, h), :],
            tok_got.at[h, frame_rows(source)],
            tok_send,
            tok_recv.at[h],
            "tm",
            d,
        )

    def ret_copy(d, source, g, h):
        return remote(
            leaving.at[h, g, frame_rows(d)],
            x_home.at[:, block_of(source, h), channels(g)],
            ret_send,
            ret_recv.at[g],
            "tm",
            d,
        )

    def own_copy(g, h):
        return pltpu.make_async_copy(
            leaving.at[h, g, frame_rows(me)], x_home.at[:, block_of(me, h), channels(g)], ret_recv.at[g]
        )

    def own_tok(h):
        return pltpu.make_async_copy(
            tok_hbm.at[:, block_of(lax.rem(me, holders), h), :],
            tok_got.at[h, frame_rows(me)],
            tok_recv.at[h],
        )

    def tot_copy(s, slot):
        return remote(
            tot_mine.at[s // halves], tot_got.at[slot], tot_send, tot_recv, "space", s
        )

    def state_copy(s, slot, g):
        return remote(
            end.at[g, s], got.at[g, slot], st_send, st_recv.at[g], "space", s
        )

    def back_copy(s, slot, g):
        return remote(
            going.at[g, s], entering.at[g, slot], back_send, back_recv.at[g], "space", s
        )

    def wait_bytes(ref, sem):
        pltpu.make_async_copy(ref, ref, sem).wait()

    others = pl.ds(0, n_space - 1)
    barrier = pltpu.get_barrier_semaphore()
    for step in range(1, n):
        pl.semaphore_signal(
            barrier,
            inc=1,
            device_id={"tm": lax.rem(me + step, n)},
            device_id_type=pl.DeviceIdType.MESH,
        )
    for step in range(1, n_space):
        pl.semaphore_signal(
            barrier,
            inc=1,
            device_id={"space": lax.rem(here + step, n_space)},
            device_id_type=pl.DeviceIdType.MESH,
        )
    pl.semaphore_wait(barrier, n + n_space - 2)

    def send_tokens(i, carry):
        h = i // (n - 1)
        d = lax.rem(me + 1 + lax.rem(i, n - 1), n)

        @pl.when(d < holders)
        def _():
            tok_copy(d, me, h).start()

        return carry

    lax.fori_loop(0, ROUNDS * (n - 1), send_tokens, 0)

    @pl.when(me < holders)
    def _():
        for h in range(ROUNDS):
            own_tok(h).start()

    spread[...] = head_spread()
    skips[...] = widen(
        jnp.concatenate(
            [
                jnp.broadcast_to(skip_t_ref[...], (8, HEADS)),
                jnp.broadcast_to(skip_s_ref[...], (8, HEADS)),
            ],
            axis=0,
        ),
        spread,
    )
    square[...] = jnp.zeros_like(square)
    acc[...] = jnp.zeros_like(acc)
    lane_low = lax.broadcasted_iota(jnp.int32, (1, 2 * CHUNK), 1) < CHUNK
    tok_load.wait()
    wt_load.wait()
    wz_load.wait()

    def home(f, carry):
        tok = tok_v[f]
        z_v[f] = nt(tok, wz[...]).astype(BF16)
        tail = nt(tok, wt[...])
        inject = tail[:, 2 * STATE : 3 * STATE].astype(BF16)
        readout = tail[:, 3 * STATE : 4 * STATE].astype(BF16)
        step = softplus(tail[:, 4 * STATE + HEADS : 4 * STATE + 2 * HEADS] + bias_s_ref[...])
        pad = padded - seq
        inject = jnp.concatenate([inject, jnp.zeros((pad, STATE), BF16)], axis=0)
        readout = jnp.concatenate([readout, jnp.zeros((pad, STATE), BF16)], axis=0)
        step = jnp.concatenate([step, jnp.zeros((pad, HEADS), F32)], axis=0)
        small_s[f] = jnp.concatenate([inject, readout], axis=1)
        log_decay = -jnp.exp(alog_s_ref[...]) * step
        offset = jnp.zeros((8, HEADS), F32)
        for k in range(count):
            rows = pl.ds(k * CHUNK, CHUNK)
            part_k = slice(k * CHUNK, (k + 1) * CHUNK)
            cum = chunk_cumsum(log_decay[part_k])
            tail_k = jnp.exp(cum[CHUNK - 1 :, :] - cum) * step[part_k]
            tail_s[f, rows, :] = split3(tail_k)[:, : 2 * HEADS]
            grown_s[f, rows, :] = split3(jnp.exp(cum))
            both = widen(jnp.concatenate([jnp.exp(last_row(cum)), jnp.exp(offset)], axis=0), spread)
            rate_s[f, pl.ds(8 * k, 8), :] = both[:8]
            reach_s[f, pl.ds(8 * k, 8), :] = both[8:]
            offset = offset + last_row(cum)
            turned_s[k] = row_forms(cum, step[part_k])
            cum_s[...] = mm(split3(cum), spread[...])
            scores2 = masked_scores(readout[part_k], inject[part_k])
            for j in range(HEADS // 2):
                lanes = pl.ds(j * 128, 128)
                w_v[f, rows, lanes] = decay_weights(cum_s[:, lanes], turned_s.at[k], scores2, j, lane_low)
        tot_mine[f] = jnp.concatenate([offset, jnp.zeros((8, 128 - HEADS), F32)], axis=1)
        for half in range(halves):
            s = halves * f + half

            @pl.when(s != here)
            def _():
                tot_copy(s, here).start()

            @pl.when(s == here)
            def _():
                tot_got[here] = tot_mine[f]

        return carry

    lax.fori_loop(0, frames, home, 0)
    wo_load.start()
    wx_load.wait()

    def prepare_round(h):
        wait_bytes(tok_got.at[h], tok_recv.at[h])
        tail = rounded(nt(tok_got[h].reshape(total * HALF, D), wt[...]))
        small_t[0] = tail[:, : 2 * STATE]
        small_t[1] = jnp.concatenate(
            [tail[:, 4 * STATE :], jnp.zeros((total * HALF, 128 - 2 * HEADS), F32)], axis=1
        )
        rate = -jnp.exp(alog_t_ref[...])

        def prepare(q, carry):
            several = [q * TOGETHER + u for u in range(TOGETHER)]
            rows = [pl.ds(p, CHUNK, stride=HALF) for p in several]
            pairs = [small_t[0, r, :].astype(BF16) for r in rows]
            steps = [softplus(small_t[1, r, :][:, :HEADS] + bias_t_ref[...]) for r in rows]
            scores = [masked_scores(pair[:, STATE:], pair[:, :STATE]) for pair in pairs]
            cums = [chunk_cumsum(rate * step) for step in steps]
            forms = [row_forms(cum, step) for cum, step in zip(cums, steps)]
            for u, p in enumerate(several):
                scores_t[p] = scores[u]
                turned_t[p] = forms[u]
                cum3[p] = split3(cums[u])
            return carry

        lax.fori_loop(0, HALF // TOGETHER, prepare, 0)

    def take_totals():
        wait_bytes(tot_got.at[others], tot_recv)
        totals = jnp.concatenate([tot_got[s] for s in range(n_space)], axis=0)[:, :HEADS]
        growth[...] = widen(jnp.exp(totals), spread)
        wo_load.wait()

    def scan_group(g, h):
        x = rounded(nt(tok_got[h].reshape(total * HALF, D), wx[channels(g), :]))
        cum = mm(cum3[...].reshape(HALF * CHUNK, 3 * HEADS), spread[:, channels(g)])
        for jj in range(PAIRS):
            x_group[jj] = x[:, jj * 128 : (jj + 1) * 128]
            cum_group[jj] = cum[:, jj * 128 : (jj + 1) * 128]

        def item(q, inner):
            work = [(q * TOGETHER + u, jj) for u in range(TOGETHER) for jj in range(PAIRS)]
            weights = [
                decay_weights(
                    cum_group[jj, pl.ds(pl.multiple_of(p * CHUNK, CHUNK), CHUNK), :],
                    turned_t.at[p],
                    scores_t[p],
                    g * PAIRS + jj,
                    lane_low,
                )
                for p, jj in work
            ]
            inputs = [x_group[jj, pl.ds(p, CHUNK, stride=HALF), :] for p, jj in work]
            mixed = [mm(w, block_pair(x.astype(BF16))) for w, x in zip(weights, inputs)]
            for u, (p, jj) in enumerate(work):
                skip = skips[pl.ds(0, 1), pair_lanes(g * PAIRS + jj)]
                out_group[jj, pl.ds(p, CHUNK, stride=HALF), :] = mixed[u] + skip * inputs[u]
            return inner

        lax.fori_loop(0, HALF // TOGETHER, item, 0)
        for jj in range(PAIRS):
            leaving[h, g, :, :, pl.ds(jj * 128, 128)] = (
                out_group[jj].astype(BF16).reshape(total, HALF, 128)
            )

        def send(step, inner):
            ret_copy(lax.rem(me + step, n), me, g, h).start()
            return inner

        lax.fori_loop(1, n, send, 0)
        own_copy(g, h).start()

    def states(g):
        wait_bytes(x_home.at[:, :, channels(g)], ret_recv.at[g])
        pieces = [(f, k, min(CHUNK, seq - k * CHUNK)) for f in range(frames) for k in range(count)]
        added = []
        for f, k, size in pieces:
            rows = pl.ds(k * CHUNK, size)
            tail_wide = mm(tail_s[f, rows, :], spread[: 2 * HEADS, channels(g)])
            weighted = (x_home[f, rows, channels(g)].astype(F32) * tail_wide).astype(BF16)
            added.append(tn(small_s[f, rows, :STATE], weighted))
        for f in range(frames):
            state = jnp.zeros((STATE, GROUP), F32)
            for k in range(count):
                starts[f, pl.ds(k * STATE, STATE), channels(g)] = state.astype(BF16)
                state = rate_s[f, pl.ds(8 * k, 1), channels(g)] * state + added[f * count + k]
            for half in range(halves):
                end[g, halves * f + half] = state[half * part : (half + 1) * part].astype(BF16)

        def send_state(step, carry):
            state_copy(lax.rem(here + step, n_space), here, g).start()
            return carry

        lax.fori_loop(1, n_space, send_state, 0)
        got[g, here] = end[g, here]

    def relay(g):
        wait_bytes(got.at[g, others], st_recv.at[g])
        running = jnp.zeros((part, GROUP), F32)
        for s in range(n_space):
            going[g, s] = running.astype(BF16)
            running = growth[pl.ds(8 * s, 1), channels(g)] * running + got[g, s].astype(F32)

        def send_back(step, carry):
            back_copy(lax.rem(here + step, n_space), here, g).start()
            return carry

        lax.fori_loop(1, n_space, send_back, 0)
        entering[g, here] = going[g, here]

    def finish(g):
        wait_bytes(entering.at[g, others], back_recv.at[g])

        def frame(f, carry):
            arrived = jnp.concatenate(
                [entering[g, halves * f + half] for half in range(halves)], axis=0
            ).astype(F32)
            sizes = [min(CHUNK, seq - k * CHUNK) for k in range(count)]
            carried, mixed = [], []
            for k, size in enumerate(sizes):
                rows = pl.ds(k * CHUNK, size)
                reach = reach_s[f, pl.ds(8 * k, 1), channels(g)]
                state = starts[f, pl.ds(k * STATE, STATE), channels(g)].astype(F32) + reach * arrived
                product = mm(small_s[f, rows, STATE:], state.astype(BF16))
                carried.append(product * mm(grown_s[f, rows, :], spread[:, channels(g)]))
                for jj in range(PAIRS):
                    lanes = pair_lanes(g * PAIRS + jj)
                    full = x_home[f, rows, lanes]
                    if size < CHUNK:
                        full = jnp.concatenate([full, jnp.zeros((CHUNK - size, 128), BF16)], axis=0)
                    mixed.append(mm(w_v[f, rows, lanes], block_pair(full)))
            for k, size in enumerate(sizes):
                rows = pl.ds(k * CHUNK, size)
                energy = square[f, rows, :]
                for jj in range(PAIRS):
                    lanes = pair_lanes(g * PAIRS + jj)
                    y = mixed[k * PAIRS + jj] + carried[k][:, jj * 128 : (jj + 1) * 128]
                    y = y + skips[pl.ds(8, 1), lanes] * x_home[f, rows, lanes].astype(F32)
                    z = z_v[f, rows, lanes].astype(F32)
                    y = y * (z * (1.0 / (1.0 + jnp.exp(-z))))
                    energy = energy + y * y
                    y_v[f, rows, pl.ds(jj * 128, 128)] = (y * gain_ref[:, lanes]).astype(BF16)
                square[f, rows, :] = energy
            return carry

        lax.fori_loop(0, frames, frame, 0)
        y_all = y_v[...].reshape(frames * seq, GROUP)
        acc[...] += mm(y_all, wz[channels(g), :])

    first = (ROUNDS - 1) * groups + LAG

    def advance(i, carry):
        g = lax.rem(i, groups)
        h = i // groups
        scanning = jnp.logical_and(i < ROUNDS * groups, me < holders)

        @pl.when(jnp.logical_and(scanning, g == 0))
        def _():
            prepare_round(h)

        @pl.when(scanning)
        def _():
            scan_group(g, h)

        @pl.when(i == first)
        def _():
            take_totals()

        @pl.when(jnp.logical_and(i >= first, i < first + groups))
        def _():
            states(i - first)

        @pl.when(jnp.logical_and(i >= first + 1, i < first + 1 + groups))
        def _():
            relay(i - first - 1)

        @pl.when(i >= first + 2)
        def _():
            finish(i - first - 2)

        return carry

    lax.fori_loop(0, first + 2 + groups, advance, 0)

    def close(f, carry):
        mean = jnp.sum(square[f], axis=1, keepdims=True) * (1.0 / DI)
        scale = lax.rsqrt(mean + 1e-5)
        product = acc[pl.ds(pl.multiple_of(f * seq, 16), seq), :]
        out_ref[f] = (product * scale + tok_v[f].astype(F32)).astype(BF16)
        return carry

    lax.fori_loop(0, frames, close, 0)

    @pl.when(me < holders)
    def _():
        wait_bytes(tok_got.at[:, pl.ds(0, frames * (holders - 1))], tok_send)
        wait_bytes(leaving.at[:, :, pl.ds(0, frames * (n - 1))], ret_send)

    @pl.when(me >= holders)
    def _():
        wait_bytes(tok_got.at[:, pl.ds(0, frames * holders)], tok_send)

    wait_bytes(tot_got.at[others], tot_send)
    wait_bytes(end.at[:, others], st_send)
    wait_bytes(going.at[:, others], back_send)


def block(tok, w_turned, w_out, bias_t, alog_t, skip_t, bias_s, alog_s, skip_s, gain):
    n = lax.axis_size("tm")
    n_space = lax.axis_size("space")
    frames, seq = tok.shape[0], tok.shape[1]
    padded = -(-seq // CHUNK) * CHUNK
    count = padded // CHUNK
    total = n * frames
    groups = DI // GROUP
    part = frames * STATE // n_space
    tail = w_turned.shape[0] - 2 * DI
    anywhere = pl.BlockSpec(memory_space=pl.ANY)
    in_vmem = pl.BlockSpec(memory_space=pltpu.VMEM)
    dma = pltpu.SemaphoreType.DMA
    vmem = pltpu.VMEM
    return pl.pallas_call(
        functools.partial(block_kernel, n, n_space),
        out_shape=jax.ShapeDtypeStruct((frames, seq, D), BF16),
        in_specs=[anywhere] * 3 + [in_vmem] * 7,
        out_specs=in_vmem,
        scratch_shapes=[
            vmem((frames, seq, D), BF16),
            vmem((ROUNDS, total, HALF, D), BF16),
            vmem((DI, D), BF16),
            vmem((DI, D), BF16),
            vmem((tail, D), BF16),
            vmem((frames, seq, DI), BF16),
            vmem((frames, padded, DI), BF16),
            vmem((PAIRS, total * HALF, 128), F32),
            vmem((PAIRS, total * HALF, 128), F32),
            vmem((PAIRS, total * HALF, 128), F32),
            vmem((ROUNDS, groups, total, HALF, GROUP), BF16),
            vmem((2, total * HALF, 128), F32),
            vmem((HALF, 128, 128), F32),
            vmem((count, 128, 128), F32),
            vmem((HALF, CHUNK, 128), F32),
            vmem((HALF, CHUNK, 3 * HEADS), BF16),
            vmem((CHUNK, DI), F32),
            vmem((3 * HEADS, DI), BF16),
            vmem((16, DI), F32),
            vmem((frames, padded, 2 * STATE), BF16),
            vmem((frames, padded, 2 * HEADS), BF16),
            vmem((frames, padded, 3 * HEADS), BF16),
            vmem((frames, 8 * count, DI), F32),
            vmem((frames, 8 * count, DI), F32),
            vmem((frames, seq, DI), BF16),
            vmem((frames, 8, 128), F32),
            vmem((n_space, 8, 128), F32),
            vmem((n_space * 8, DI), F32),
            vmem((frames, count * STATE, DI), BF16),
            vmem((groups, n_space, part, GROUP), BF16),
            vmem((groups, n_space, part, GROUP), BF16),
            vmem((groups, n_space, part, GROUP), BF16),
            vmem((groups, n_space, part, GROUP), BF16),
            vmem((frames, seq, GROUP), BF16),
            vmem((frames, seq, 128), F32),
            vmem((frames * seq, D), F32),
            dma((5,)),
            dma(()),
            dma((ROUNDS,)),
            dma(()),
            dma((groups,)),
            dma(()),
            dma(()),
            dma(()),
            dma((groups,)),
            dma(()),
            dma((groups,)),
        ],
        compiler_params=pltpu.CompilerParams(
            collective_id=0, has_side_effects=True, vmem_limit_bytes=60 * MIB
        ),
    )(tok, w_turned, w_out, bias_t, alog_t, skip_t, bias_s, alog_s, skip_s, gain)


def body(
    tokens,
    w_in,
    w_out,
    a_log_time,
    a_log_space,
    dt_bias_time,
    dt_bias_space,
    skip_time,
    skip_space,
    norm_gain,
):
    frames = tokens.shape[0]
    tok = tokens.reshape(frames, -1, D)
    one = lambda v: v.reshape(1, -1)
    out = block(
        tok,
        w_in.T,
        w_out,
        one(dt_bias_time),
        one(a_log_time),
        one(skip_time),
        one(dt_bias_space),
        one(a_log_space),
        one(skip_space),
        one(norm_gain),
    )
    return out.reshape(tokens.shape)


def solution(mesh):
    placed = (P("tm", "space", None, None), P(), P(), P(), P(), P(), P(), P(), P(), P())
    return jax.shard_map(
        body, mesh=mesh, in_specs=placed, out_specs=P("tm", "space", None, None), check_vma=False
    )
```

```python
import functools

import jax
import jax.numpy as jnp
from jax import lax
from jax.experimental import pallas as pl
from jax.experimental.pallas import tpu as pltpu
from jax.sharding import PartitionSpec as P

D = 1024
HEADS = 32
HEAD_DIM = 64
STATE = 64
DI = 2048
CHUNK = 64
F32 = jnp.float32
BF16 = jnp.bfloat16
MIB = 1 << 20


def mm(a, b):
    return jnp.dot(a, b, preferred_element_type=F32)


def softplus(v):
    return jnp.maximum(v, 0.0) + jnp.log1p(jnp.exp(-jnp.abs(v)))


def split3(v):
    hi = v.astype(BF16)
    rest = v - hi.astype(F32)
    mid = rest.astype(BF16)
    low = (rest - mid.astype(F32)).astype(BF16)
    return jnp.concatenate([hi, mid, low], axis=1)


def head_spread():
    row = lax.broadcasted_iota(jnp.int32, (3 * HEADS, DI), 0) % HEADS
    col = lax.broadcasted_iota(jnp.int32, (3 * HEADS, DI), 1) // HEAD_DIM
    return (row == col).astype(BF16)


def causal_ones():
    row = lax.broadcasted_iota(jnp.int32, (CHUNK, CHUNK), 0)
    col = lax.broadcasted_iota(jnp.int32, (CHUNK, CHUNK), 1)
    return row >= col


def chunk_cumsum(log_decay):
    tri = causal_ones().astype(F32).astype(BF16)
    wide = mm(tri, split3(log_decay))
    return wide[:, :HEADS] + wide[:, HEADS : 2 * HEADS] + wide[:, 2 * HEADS :]


def row_forms(cum, step):
    pair = jnp.concatenate([cum, step, jnp.zeros((CHUNK, 2 * HEADS), F32)], axis=1)
    return jnp.concatenate([pair, pair], axis=0).T


def pair_rows(turned_ref, base, j, lane_low):
    even = turned_ref[pl.ds(base + 2 * j, 1), :]
    odd = turned_ref[pl.ds(base + 2 * j + 1, 1), :]
    return jnp.where(lane_low, even, odd)


def decay_weights(cum_wide, turned_ref, scores2, j, lane_low):
    cum_row = pair_rows(turned_ref, 0, j, lane_low)
    step_row = pair_rows(turned_ref, HEADS, j, lane_low)
    span = jnp.exp(jnp.minimum(cum_wide - cum_row, 0.0))
    return (span * (scores2 * step_row)).astype(BF16)


def masked_scores(readout, inject):
    scores = lax.dot_general(readout, inject, (((1,), (1,)), ((), ())), preferred_element_type=F32)
    scores = jnp.where(causal_ones(), scores, 0.0)
    return jnp.concatenate([scores, scores], axis=1)


def block_pair(x_pair):
    low = lax.broadcasted_iota(jnp.int32, x_pair.shape, 1) < HEAD_DIM
    zero = jnp.zeros_like(x_pair)
    return jnp.concatenate([jnp.where(low, x_pair, zero), jnp.where(low, zero, x_pair)], axis=0)


ITEMS = 16
GROUP = 512
PAIRS = GROUP // 128
TOGETHER = 4
NARROW = 256
RELAY_LAG = 2
FINISH_LAG = 4
NPAIRS = NARROW // 128
HALF = 8
ROUNDS = ITEMS // HALF


def nt(a, b):
    return lax.dot_general(a, b, (((1,), (1,)), ((), ())), preferred_element_type=F32)


def tn(a, b):
    return lax.dot_general(a, b, (((0,), (0,)), ((), ())), preferred_element_type=F32)


def rounded(v):
    return v.astype(BF16).astype(F32)


def widen(values, spread):
    return mm(split3(values), spread[...])


def last_row(values):
    return jnp.broadcast_to(values[CHUNK - 1 :, :], (8, HEADS))


def block_kernel(
    n,
    n_space,
    tok_hbm,
    w_hbm,
    wo_hbm,
    bias_t_ref,
    alog_t_ref,
    skip_t_ref,
    bias_s_ref,
    alog_s_ref,
    skip_s_ref,
    gain_ref,
    out_ref,
    tok_v,
    tok_got,
    wz,
    wx,
    wt,
    z_v,
    w_v,
    x_group,
    cum_group,
    out_group,
    leaving,
    small_t,
    turned_t,
    turned_s,
    scores_t,
    cum3,
    cum_s,
    spread,
    skips,
    small_s,
    tail_s,
    grown_s,
    rate_s,
    reach_s,
    x_home,
    tot_mine,
    tot_got,
    growth,
    starts,
    end,
    got,
    going,
    entering,
    y_v,
    square,
    acc,
    load_sem,
    tok_send,
    tok_recv,
    ret_send,
    ret_recv,
    tot_send,
    tot_recv,
    st_send,
    st_recv,
    back_send,
    back_recv,
):
    frames, seq = tok_v.shape[0], tok_v.shape[1]
    padded = w_v.shape[1]
    count = padded // CHUNK
    holders = seq // ITEMS
    total = n * frames
    groups = DI // GROUP
    narrow_groups = DI // NARROW
    halves = n_space // frames
    part = STATE // halves
    me = lax.axis_index("tm")
    here = lax.axis_index("space")

    tok_load = pltpu.make_async_copy(tok_hbm, tok_v, load_sem.at[0])
    wz_load = pltpu.make_async_copy(w_hbm.at[pl.ds(0, DI)], wz, load_sem.at[1])
    wt_load = pltpu.make_async_copy(w_hbm.at[pl.ds(2 * DI, wt.shape[0])], wt, load_sem.at[2])
    wx_load = pltpu.make_async_copy(w_hbm.at[pl.ds(DI, DI)], wx, load_sem.at[3])
    wo_load = pltpu.make_async_copy(wo_hbm, wz, load_sem.at[4])
    tok_load.start()
    wt_load.start()
    wz_load.start()
    wx_load.start()

    def remote(src, dst, send, recv, axis, device):
        return pltpu.make_async_remote_copy(
            src_ref=src,
            dst_ref=dst,
            send_sem=send,
            recv_sem=recv,
            device_id={axis: device},
            device_id_type=pl.DeviceIdType.MESH,
        )

    def frame_rows(d):
        return pl.ds(d * frames, frames)

    def channels(g):
        return pl.ds(pl.multiple_of(g * GROUP, GROUP), GROUP)

    def narrow(g):
        return pl.ds(pl.multiple_of(g * NARROW, NARROW), NARROW)

    def pair_lanes(j):
        return pl.ds(pl.multiple_of(j * 128, 128), 128)

    def block_of(d, h):
        return pl.ds(pl.multiple_of(d * ITEMS + h * HALF, HALF), HALF)

    def tok_copy(d, source, h):
        return remote(
            tok_hbm.at[:, block_of(d, h), :],
            tok_got.at[h, frame_rows(source)],
            tok_send,
            tok_recv.at[h],
            "tm",
            d,
        )

    def ret_copy(d, source, g, h):
        return remote(
            leaving.at[h, g, frame_rows(d)],
            x_home.at[:, block_of(source, h), channels(g)],
            ret_send,
            ret_recv.at[g],
            "tm",
            d,
        )

    def own_copy(g, h):
        return pltpu.make_async_copy(
            leaving.at[h, g, frame_rows(me)], x_home.at[:, block_of(me, h), channels(g)], ret_recv.at[g]
        )

    def own_tok(h):
        return pltpu.make_async_copy(
            tok_hbm.at[:, block_of(lax.rem(me, holders), h), :],
            tok_got.at[h, frame_rows(me)],
            tok_recv.at[h],
        )

    def tot_copy(s, slot):
        return remote(
            tot_mine.at[s // halves], tot_got.at[slot], tot_send, tot_recv, "space", s
        )

    def state_copy(s, slot, g):
        return remote(
            end.at[g, s], got.at[g, slot], st_send, st_recv.at[g], "space", s
        )

    def back_copy(s, slot, g):
        return remote(
            going.at[g, s], entering.at[g, slot], back_send, back_recv.at[g], "space", s
        )

    def wait_bytes(ref, sem):
        pltpu.make_async_copy(ref, ref, sem).wait()

    others = pl.ds(0, n_space - 1)
    barrier = pltpu.get_barrier_semaphore()
    for step in range(1, n):
        pl.semaphore_signal(
            barrier,
            inc=1,
            device_id={"tm": lax.rem(me + step, n)},
            device_id_type=pl.DeviceIdType.MESH,
        )
    for step in range(1, n_space):
        pl.semaphore_signal(
            barrier,
            inc=1,
            device_id={"space": lax.rem(here + step, n_space)},
            device_id_type=pl.DeviceIdType.MESH,
        )
    pl.semaphore_wait(barrier, n + n_space - 2)

    def send_tokens(i, carry):
        h = i // (n - 1)
        d = lax.rem(me + 1 + lax.rem(i, n - 1), n)

        @pl.when(d < holders)
        def _():
            tok_copy(d, me, h).start()

        return carry

    lax.fori_loop(0, ROUNDS * (n - 1), send_tokens, 0)

    @pl.when(me < holders)
    def _():
        for h in range(ROUNDS):
            own_tok(h).start()

    spread[...] = head_spread()
    skips[...] = widen(
        jnp.concatenate(
            [
                jnp.broadcast_to(skip_t_ref[...], (8, HEADS)),
                jnp.broadcast_to(skip_s_ref[...], (8, HEADS)),
            ],
            axis=0,
        ),
        spread,
    )
    square[...] = jnp.zeros_like(square)
    acc[...] = jnp.zeros_like(acc)
    lane_low = lax.broadcasted_iota(jnp.int32, (1, 2 * CHUNK), 1) < CHUNK
    tok_load.wait()
    wt_load.wait()
    wz_load.wait()

    def home(f, carry):
        tok = tok_v[f]
        z_v[f] = nt(tok, wz[...]).astype(BF16)
        tail = nt(tok, wt[...])
        inject = tail[:, 2 * STATE : 3 * STATE].astype(BF16)
        readout = tail[:, 3 * STATE : 4 * STATE].astype(BF16)
        step = softplus(tail[:, 4 * STATE + HEADS : 4 * STATE + 2 * HEADS] + bias_s_ref[...])
        pad = padded - seq
        inject = jnp.concatenate([inject, jnp.zeros((pad, STATE), BF16)], axis=0)
        readout = jnp.concatenate([readout, jnp.zeros((pad, STATE), BF16)], axis=0)
        step = jnp.concatenate([step, jnp.zeros((pad, HEADS), F32)], axis=0)
        small_s[f] = jnp.concatenate([inject, readout], axis=1)
        log_decay = -jnp.exp(alog_s_ref[...]) * step
        offset = jnp.zeros((8, HEADS), F32)
        for k in range(count):
            rows = pl.ds(k * CHUNK, CHUNK)
            part_k = slice(k * CHUNK, (k + 1) * CHUNK)
            cum = chunk_cumsum(log_decay[part_k])
            tail_k = jnp.exp(cum[CHUNK - 1 :, :] - cum) * step[part_k]
            tail_s[f, rows, :] = split3(tail_k)[:, : 2 * HEADS]
            grown_s[f, rows, :] = split3(jnp.exp(cum))
            both = widen(jnp.concatenate([jnp.exp(last_row(cum)), jnp.exp(offset)], axis=0), spread)
            rate_s[f, pl.ds(8 * k, 8), :] = both[:8]
            reach_s[f, pl.ds(8 * k, 8), :] = both[8:]
            offset = offset + last_row(cum)
            turned_s[k] = row_forms(cum, step[part_k])
            cum_s[...] = mm(split3(cum), spread[...])
            scores2 = masked_scores(readout[part_k], inject[part_k])
            for j in range(HEADS // 2):
                lanes = pl.ds(j * 128, 128)
                w_v[f, rows, lanes] = decay_weights(cum_s[:, lanes], turned_s.at[k], scores2, j, lane_low)
        tot_mine[f] = jnp.concatenate([offset, jnp.zeros((8, 128 - HEADS), F32)], axis=1)
        for half in range(halves):
            s = halves * f + half

            @pl.when(s != here)
            def _():
                tot_copy(s, here).start()

            @pl.when(s == here)
            def _():
                tot_got[here] = tot_mine[f]

        return carry

    lax.fori_loop(0, frames, home, 0)
    wo_load.start()
    wx_load.wait()

    def prepare_round(h):
        wait_bytes(tok_got.at[h], tok_recv.at[h])
        tail = rounded(nt(tok_got[h].reshape(total * HALF, D), wt[...]))
        small_t[0] = tail[:, : 2 * STATE]
        small_t[1] = jnp.concatenate(
            [tail[:, 4 * STATE :], jnp.zeros((total * HALF, 128 - 2 * HEADS), F32)], axis=1
        )
        rate = -jnp.exp(alog_t_ref[...])

        def prepare(q, carry):
            several = [q * TOGETHER + u for u in range(TOGETHER)]
            rows = [pl.ds(p, CHUNK, stride=HALF) for p in several]
            pairs = [small_t[0, r, :].astype(BF16) for r in rows]
            steps = [softplus(small_t[1, r, :][:, :HEADS] + bias_t_ref[...]) for r in rows]
            scores = [masked_scores(pair[:, STATE:], pair[:, :STATE]) for pair in pairs]
            cums = [chunk_cumsum(rate * step) for step in steps]
            forms = [row_forms(cum, step) for cum, step in zip(cums, steps)]
            for u, p in enumerate(several):
                scores_t[p] = scores[u]
                turned_t[p] = forms[u]
                cum3[p] = split3(cums[u])
            return carry

        lax.fori_loop(0, HALF // TOGETHER, prepare, 0)

    def take_totals():
        wait_bytes(tot_got.at[others], tot_recv)
        totals = jnp.concatenate([tot_got[s] for s in range(n_space)], axis=0)[:, :HEADS]
        growth[...] = widen(jnp.exp(totals), spread)
        wo_load.wait()

    def scan_group(g, h):
        x = rounded(nt(tok_got[h].reshape(total * HALF, D), wx[channels(g), :]))
        cum = mm(cum3[...].reshape(HALF * CHUNK, 3 * HEADS), spread[:, channels(g)])
        for jj in range(PAIRS):
            x_group[jj] = x[:, jj * 128 : (jj + 1) * 128]
            cum_group[jj] = cum[:, jj * 128 : (jj + 1) * 128]

        def item(q, inner):
            work = [(q * TOGETHER + u, jj) for u in range(TOGETHER) for jj in range(PAIRS)]
            weights = [
                decay_weights(
                    cum_group[jj, pl.ds(pl.multiple_of(p * CHUNK, CHUNK), CHUNK), :],
                    turned_t.at[p],
                    scores_t[p],
                    g * PAIRS + jj,
                    lane_low,
                )
                for p, jj in work
            ]
            inputs = [x_group[jj, pl.ds(p, CHUNK, stride=HALF), :] for p, jj in work]
            mixed = [mm(w, block_pair(x.astype(BF16))) for w, x in zip(weights, inputs)]
            for u, (p, jj) in enumerate(work):
                skip = skips[pl.ds(0, 1), pair_lanes(g * PAIRS + jj)]
                out_group[jj, pl.ds(p, CHUNK, stride=HALF), :] = mixed[u] + skip * inputs[u]
            return inner

        lax.fori_loop(0, HALF // TOGETHER, item, 0)
        for jj in range(PAIRS):
            leaving[h, g, :, :, pl.ds(jj * 128, 128)] = (
                out_group[jj].astype(BF16).reshape(total, HALF, 128)
            )

        def send(step, inner):
            ret_copy(lax.rem(me + step, n), me, g, h).start()
            return inner

        lax.fori_loop(1, n, send, 0)
        own_copy(g, h).start()

    def states(g):
        whole = lax.div(g, GROUP // NARROW)

        @pl.when(lax.rem(g, GROUP // NARROW) == 0)
        def _():
            wait_bytes(x_home.at[:, :, channels(whole)], ret_recv.at[whole])

        pieces = [(f, k, min(CHUNK, seq - k * CHUNK)) for f in range(frames) for k in range(count)]
        added = []
        for f, k, size in pieces:
            rows = pl.ds(k * CHUNK, size)
            tail_wide = mm(tail_s[f, rows, :], spread[: 2 * HEADS, narrow(g)])
            weighted = (x_home[f, rows, narrow(g)].astype(F32) * tail_wide).astype(BF16)
            added.append(tn(small_s[f, rows, :STATE], weighted))
        for f in range(frames):
            state = jnp.zeros((STATE, NARROW), F32)
            for k in range(count):
                starts[f, pl.ds(k * STATE, STATE), narrow(g)] = state.astype(BF16)
                state = rate_s[f, pl.ds(8 * k, 1), narrow(g)] * state + added[f * count + k]
            for half in range(halves):
                end[g, halves * f + half] = state[half * part : (half + 1) * part].astype(BF16)

        def send_state(step, carry):
            state_copy(lax.rem(here + step, n_space), here, g).start()
            return carry

        lax.fori_loop(1, n_space, send_state, 0)
        got[g, here] = end[g, here]

    def relay(g):
        wait_bytes(got.at[g, others], st_recv.at[g])
        running = jnp.zeros((part, NARROW), F32)
        for s in range(n_space):
            going[g, s] = running.astype(BF16)
            running = growth[pl.ds(8 * s, 1), narrow(g)] * running + got[g, s].astype(F32)

        def send_back(step, carry):
            back_copy(lax.rem(here + step, n_space), here, g).start()
            return carry

        lax.fori_loop(1, n_space, send_back, 0)
        entering[g, here] = going[g, here]

    def finish(g):
        wait_bytes(entering.at[g, others], back_recv.at[g])

        def frame(f, carry):
            arrived = jnp.concatenate(
                [entering[g, halves * f + half] for half in range(halves)], axis=0
            ).astype(F32)
            sizes = [min(CHUNK, seq - k * CHUNK) for k in range(count)]
            carried, mixed = [], []
            for k, size in enumerate(sizes):
                rows = pl.ds(k * CHUNK, size)
                reach = reach_s[f, pl.ds(8 * k, 1), narrow(g)]
                state = starts[f, pl.ds(k * STATE, STATE), narrow(g)].astype(F32) + reach * arrived
                product = mm(small_s[f, rows, STATE:], state.astype(BF16))
                carried.append(product * mm(grown_s[f, rows, :], spread[:, narrow(g)]))
                for jj in range(NPAIRS):
                    lanes = pair_lanes(g * NPAIRS + jj)
                    full = x_home[f, rows, lanes]
                    if size < CHUNK:
                        full = jnp.concatenate([full, jnp.zeros((CHUNK - size, 128), BF16)], axis=0)
                    mixed.append(mm(w_v[f, rows, lanes], block_pair(full)))
            for k, size in enumerate(sizes):
                rows = pl.ds(k * CHUNK, size)
                energy = square[f, rows, :]
                for jj in range(NPAIRS):
                    lanes = pair_lanes(g * NPAIRS + jj)
                    y = mixed[k * NPAIRS + jj] + carried[k][:, jj * 128 : (jj + 1) * 128]
                    y = y + skips[pl.ds(8, 1), lanes] * x_home[f, rows, lanes].astype(F32)
                    z = z_v[f, rows, lanes].astype(F32)
                    y = y * (z * (1.0 / (1.0 + jnp.exp(-z))))
                    energy = energy + y * y
                    y_v[f, rows, pl.ds(jj * 128, 128)] = (y * gain_ref[:, lanes]).astype(BF16)
                square[f, rows, :] = energy
            return carry

        lax.fori_loop(0, frames, frame, 0)
        y_all = y_v[...].reshape(frames * seq, NARROW)
        acc[...] += mm(y_all, wz[narrow(g), :])

    @pl.when(me < holders)
    def _():
        def scan(i, carry):
            g = lax.rem(i, groups)
            h = i // groups

            @pl.when(g == 0)
            def _():
                prepare_round(h)

            scan_group(g, h)
            return carry

        lax.fori_loop(0, ROUNDS * groups, scan, 0)

    take_totals()

    def advance(i, carry):
        @pl.when(i < narrow_groups)
        def _():
            states(i)

        @pl.when(jnp.logical_and(i >= RELAY_LAG, i < narrow_groups + RELAY_LAG))
        def _():
            relay(i - RELAY_LAG)

        @pl.when(i >= FINISH_LAG)
        def _():
            finish(i - FINISH_LAG)

        return carry

    lax.fori_loop(0, narrow_groups + FINISH_LAG, advance, 0)

    def close(f, carry):
        mean = jnp.sum(square[f], axis=1, keepdims=True) * (1.0 / DI)
        scale = lax.rsqrt(mean + 1e-5)
        product = acc[pl.ds(pl.multiple_of(f * seq, 16), seq), :]
        out_ref[f] = (product * scale + tok_v[f].astype(F32)).astype(BF16)
        return carry

    lax.fori_loop(0, frames, close, 0)

    @pl.when(me < holders)
    def _():
        wait_bytes(tok_got.at[:, pl.ds(0, frames * (holders - 1))], tok_send)
        wait_bytes(leaving.at[:, :, pl.ds(0, frames * (n - 1))], ret_send)

    @pl.when(me >= holders)
    def _():
        wait_bytes(tok_got.at[:, pl.ds(0, frames * holders)], tok_send)

    wait_bytes(tot_got.at[others], tot_send)
    wait_bytes(end.at[:, others], st_send)
    wait_bytes(going.at[:, others], back_send)


def block(tok, w_turned, w_out, bias_t, alog_t, skip_t, bias_s, alog_s, skip_s, gain):
    n = lax.axis_size("tm")
    n_space = lax.axis_size("space")
    frames, seq = tok.shape[0], tok.shape[1]
    padded = -(-seq // CHUNK) * CHUNK
    count = padded // CHUNK
    total = n * frames
    groups = DI // GROUP
    part = frames * STATE // n_space
    tail = w_turned.shape[0] - 2 * DI
    anywhere = pl.BlockSpec(memory_space=pl.ANY)
    in_vmem = pl.BlockSpec(memory_space=pltpu.VMEM)
    dma = pltpu.SemaphoreType.DMA
    vmem = pltpu.VMEM
    return pl.pallas_call(
        functools.partial(block_kernel, n, n_space),
        out_shape=jax.ShapeDtypeStruct((frames, seq, D), BF16),
        in_specs=[anywhere] * 3 + [in_vmem] * 7,
        out_specs=in_vmem,
        scratch_shapes=[
            vmem((frames, seq, D), BF16),
            vmem((ROUNDS, total, HALF, D), BF16),
            vmem((DI, D), BF16),
            vmem((DI, D), BF16),
            vmem((tail, D), BF16),
            vmem((frames, seq, DI), BF16),
            vmem((frames, padded, DI), BF16),
            vmem((PAIRS, total * HALF, 128), F32),
            vmem((PAIRS, total * HALF, 128), F32),
            vmem((PAIRS, total * HALF, 128), F32),
            vmem((ROUNDS, groups, total, HALF, GROUP), BF16),
            vmem((2, total * HALF, 128), F32),
            vmem((HALF, 128, 128), F32),
            vmem((count, 128, 128), F32),
            vmem((HALF, CHUNK, 128), F32),
            vmem((HALF, CHUNK, 3 * HEADS), BF16),
            vmem((CHUNK, DI), F32),
            vmem((3 * HEADS, DI), BF16),
            vmem((16, DI), F32),
            vmem((frames, padded, 2 * STATE), BF16),
            vmem((frames, padded, 2 * HEADS), BF16),
            vmem((frames, padded, 3 * HEADS), BF16),
            vmem((frames, 8 * count, DI), F32),
            vmem((frames, 8 * count, DI), F32),
            vmem((frames, seq, DI), BF16),
            vmem((frames, 8, 128), F32),
            vmem((n_space, 8, 128), F32),
            vmem((n_space * 8, DI), F32),
            vmem((frames, count * STATE, DI), BF16),
            vmem((DI // NARROW, n_space, part, NARROW), BF16),
            vmem((DI // NARROW, n_space, part, NARROW), BF16),
            vmem((DI // NARROW, n_space, part, NARROW), BF16),
            vmem((DI // NARROW, n_space, part, NARROW), BF16),
            vmem((frames, seq, NARROW), BF16),
            vmem((frames, seq, 128), F32),
            vmem((frames * seq, D), F32),
            dma((5,)),
            dma(()),
            dma((ROUNDS,)),
            dma(()),
            dma((groups,)),
            dma(()),
            dma(()),
            dma(()),
            dma((DI // NARROW,)),
            dma(()),
            dma((DI // NARROW,)),
        ],
        compiler_params=pltpu.CompilerParams(
            collective_id=0, has_side_effects=True, vmem_limit_bytes=60 * MIB
        ),
    )(tok, w_turned, w_out, bias_t, alog_t, skip_t, bias_s, alog_s, skip_s, gain)


def body(
    tokens,
    w_in,
    w_out,
    a_log_time,
    a_log_space,
    dt_bias_time,
    dt_bias_space,
    skip_time,
    skip_space,
    norm_gain,
):
    frames = tokens.shape[0]
    tok = tokens.reshape(frames, -1, D)
    one = lambda v: v.reshape(1, -1)
    out = block(
        tok,
        w_in.T,
        w_out,
        one(dt_bias_time),
        one(a_log_time),
        one(skip_time),
        one(dt_bias_space),
        one(a_log_space),
        one(skip_space),
        one(norm_gain),
    )
    return out.reshape(tokens.shape)


def solution(mesh):
    placed = (P("tm", "space", None, None), P(), P(), P(), P(), P(), P(), P(), P(), P())
    return jax.shard_map(
        body, mesh=mesh, in_specs=placed, out_specs=P("tm", "space", None, None), check_vma=False
    )
```

```python
import functools

import jax
import jax.numpy as jnp
from jax import lax
from jax.experimental import pallas as pl
from jax.experimental.pallas import tpu as pltpu
from jax.sharding import PartitionSpec as P

D = 1024
HEADS = 32
HEAD_DIM = 64
STATE = 64
DI = 2048
CHUNK = 64
F32 = jnp.float32
BF16 = jnp.bfloat16
MIB = 1 << 20


def mm(a, b):
    return jnp.dot(a, b, preferred_element_type=F32)


def softplus(v):
    return jnp.maximum(v, 0.0) + jnp.log1p(jnp.exp(-jnp.abs(v)))


def split3(v):
    hi = v.astype(BF16)
    rest = v - hi.astype(F32)
    mid = rest.astype(BF16)
    low = (rest - mid.astype(F32)).astype(BF16)
    return jnp.concatenate([hi, mid, low], axis=1)


def head_spread():
    row = lax.broadcasted_iota(jnp.int32, (3 * HEADS, DI), 0) % HEADS
    col = lax.broadcasted_iota(jnp.int32, (3 * HEADS, DI), 1) // HEAD_DIM
    return (row == col).astype(BF16)


def causal_ones():
    row = lax.broadcasted_iota(jnp.int32, (CHUNK, CHUNK), 0)
    col = lax.broadcasted_iota(jnp.int32, (CHUNK, CHUNK), 1)
    return row >= col


def chunk_cumsum(log_decay):
    tri = causal_ones().astype(F32).astype(BF16)
    wide = mm(tri, split3(log_decay))
    return wide[:, :HEADS] + wide[:, HEADS : 2 * HEADS] + wide[:, 2 * HEADS :]


def row_forms(cum, step):
    pair = jnp.concatenate([cum, step, jnp.zeros((CHUNK, 2 * HEADS), F32)], axis=1)
    return jnp.concatenate([pair, pair], axis=0).T


def pair_rows(turned_ref, base, j, lane_low):
    even = turned_ref[pl.ds(base + 2 * j, 1), :]
    odd = turned_ref[pl.ds(base + 2 * j + 1, 1), :]
    return jnp.where(lane_low, even, odd)


def decay_weights(cum_wide, turned_ref, scores2, j, lane_low):
    cum_row = pair_rows(turned_ref, 0, j, lane_low)
    step_row = pair_rows(turned_ref, HEADS, j, lane_low)
    span = jnp.exp(jnp.minimum(cum_wide - cum_row, 0.0))
    return (span * (scores2 * step_row)).astype(BF16)


def masked_scores(readout, inject):
    scores = lax.dot_general(readout, inject, (((1,), (1,)), ((), ())), preferred_element_type=F32)
    scores = jnp.where(causal_ones(), scores, 0.0)
    return jnp.concatenate([scores, scores], axis=1)


def block_pair(x_pair):
    low = lax.broadcasted_iota(jnp.int32, x_pair.shape, 1) < HEAD_DIM
    zero = jnp.zeros_like(x_pair)
    return jnp.concatenate([jnp.where(low, x_pair, zero), jnp.where(low, zero, x_pair)], axis=0)


ITEMS = 16
GROUP = 512
PAIRS = GROUP // 128
TOGETHER = 4
NARROW = 256
RELAY_LAG = 2
FINISH_LAG = 4
NPAIRS = NARROW // 128
HALF = 8
ROUNDS = ITEMS // HALF


def nt(a, b):
    return lax.dot_general(a, b, (((1,), (1,)), ((), ())), preferred_element_type=F32)


def tn(a, b):
    return lax.dot_general(a, b, (((0,), (0,)), ((), ())), preferred_element_type=F32)


def rounded(v):
    return v.astype(BF16).astype(F32)


def widen(values, spread):
    return mm(split3(values), spread[...])


def last_row(values):
    return jnp.broadcast_to(values[CHUNK - 1 :, :], (8, HEADS))


def block_kernel(
    n,
    n_space,
    tok_hbm,
    w_hbm,
    wo_hbm,
    bias_t_ref,
    alog_t_ref,
    skip_t_ref,
    bias_s_ref,
    alog_s_ref,
    skip_s_ref,
    gain_ref,
    out_ref,
    tok_v,
    tok_got,
    wz,
    wx,
    wt,
    z_v,
    w_v,
    x_group,
    cum_group,
    out_group,
    leaving,
    small_t,
    turned_t,
    turned_s,
    scores_t,
    cum3,
    cum_s,
    spread,
    skips,
    small_s,
    tail_s,
    grown_s,
    rate_s,
    reach_s,
    x_home,
    tot_mine,
    tot_got,
    growth,
    starts,
    end,
    got,
    going,
    entering,
    y_v,
    square,
    acc,
    load_sem,
    tok_send,
    tok_recv,
    ret_send,
    ret_recv,
    tot_send,
    tot_recv,
    st_send,
    st_recv,
    back_send,
    back_recv,
):
    frames, seq = tok_v.shape[0], tok_v.shape[1]
    padded = w_v.shape[1]
    count = padded // CHUNK
    holders = seq // ITEMS
    total = n * frames
    groups = DI // GROUP
    narrow_groups = DI // NARROW
    halves = n_space // frames
    part = STATE // halves
    me = lax.axis_index("tm")
    here = lax.axis_index("space")

    tok_load = pltpu.make_async_copy(tok_hbm, tok_v, load_sem.at[0])
    wz_load = pltpu.make_async_copy(w_hbm.at[pl.ds(0, DI)], wz, load_sem.at[1])
    wt_load = pltpu.make_async_copy(w_hbm.at[pl.ds(2 * DI, wt.shape[0])], wt, load_sem.at[2])
    wx_load = pltpu.make_async_copy(w_hbm.at[pl.ds(DI, DI)], wx, load_sem.at[3])
    wo_load = pltpu.make_async_copy(wo_hbm, wz, load_sem.at[4])
    tok_load.start()
    wt_load.start()
    wz_load.start()
    wx_load.start()

    def remote(src, dst, send, recv, axis, device):
        return pltpu.make_async_remote_copy(
            src_ref=src,
            dst_ref=dst,
            send_sem=send,
            recv_sem=recv,
            device_id={axis: device},
            device_id_type=pl.DeviceIdType.MESH,
        )

    def frame_rows(d):
        return pl.ds(d * frames, frames)

    def channels(g):
        return pl.ds(pl.multiple_of(g * GROUP, GROUP), GROUP)

    def narrow(g):
        return pl.ds(pl.multiple_of(g * NARROW, NARROW), NARROW)

    def pair_lanes(j):
        return pl.ds(pl.multiple_of(j * 128, 128), 128)

    def block_of(d, h):
        return pl.ds(pl.multiple_of(d * ITEMS + h * HALF, HALF), HALF)

    def tok_copy(d, source, h):
        return remote(
            tok_hbm.at[:, block_of(d, h), :],
            tok_got.at[h, frame_rows(source)],
            tok_send,
            tok_recv.at[h],
            "tm",
            d,
        )

    def ret_copy(d, source, g, h):
        return remote(
            leaving.at[h, g, frame_rows(d)],
            x_home.at[:, block_of(source, h), channels(g)],
            ret_send,
            ret_recv.at[g],
            "tm",
            d,
        )

    def own_copy(g, h):
        return pltpu.make_async_copy(
            leaving.at[h, g, frame_rows(me)], x_home.at[:, block_of(me, h), channels(g)], ret_recv.at[g]
        )

    def own_tok(h):
        return pltpu.make_async_copy(
            tok_hbm.at[:, block_of(lax.rem(me, holders), h), :],
            tok_got.at[h, frame_rows(me)],
            tok_recv.at[h],
        )

    def tot_copy(s, slot):
        return remote(
            tot_mine.at[s // halves], tot_got.at[slot], tot_send, tot_recv, "space", s
        )

    def state_copy(s, slot, g):
        return remote(
            end.at[g, s], got.at[g, slot], st_send, st_recv.at[g], "space", s
        )

    def back_copy(s, slot, g):
        return remote(
            going.at[g, s], entering.at[g, slot], back_send, back_recv.at[g], "space", s
        )

    def wait_bytes(ref, sem):
        pltpu.make_async_copy(ref, ref, sem).wait()

    others = pl.ds(0, n_space - 1)
    barrier = pltpu.get_barrier_semaphore()
    for step in range(1, n):
        pl.semaphore_signal(
            barrier,
            inc=1,
            device_id={"tm": lax.rem(me + step, n)},
            device_id_type=pl.DeviceIdType.MESH,
        )
    for step in range(1, n_space):
        pl.semaphore_signal(
            barrier,
            inc=1,
            device_id={"space": lax.rem(here + step, n_space)},
            device_id_type=pl.DeviceIdType.MESH,
        )
    pl.semaphore_wait(barrier, n + n_space - 2)

    def send_tokens(i, carry):
        h = i // (n - 1)
        d = lax.rem(me + 1 + lax.rem(i, n - 1), n)

        @pl.when(d < holders)
        def _():
            tok_copy(d, me, h).start()

        return carry

    lax.fori_loop(0, ROUNDS * (n - 1), send_tokens, 0)

    @pl.when(me < holders)
    def _():
        for h in range(ROUNDS):
            own_tok(h).start()

    spread[...] = head_spread()
    skips[...] = widen(
        jnp.concatenate(
            [
                jnp.broadcast_to(skip_t_ref[...], (8, HEADS)),
                jnp.broadcast_to(skip_s_ref[...], (8, HEADS)),
            ],
            axis=0,
        ),
        spread,
    )
    square[...] = jnp.zeros_like(square)
    acc[...] = jnp.zeros_like(acc)
    lane_low = lax.broadcasted_iota(jnp.int32, (1, 2 * CHUNK), 1) < CHUNK
    tok_load.wait()
    wt_load.wait()
    wz_load.wait()

    def home(f, carry):
        tok = tok_v[f]
        z_v[f] = nt(tok, wz[...]).astype(BF16)
        tail = nt(tok, wt[...])
        inject = tail[:, 2 * STATE : 3 * STATE].astype(BF16)
        readout = tail[:, 3 * STATE : 4 * STATE].astype(BF16)
        step = softplus(tail[:, 4 * STATE + HEADS : 4 * STATE + 2 * HEADS] + bias_s_ref[...])
        pad = padded - seq
        inject = jnp.concatenate([inject, jnp.zeros((pad, STATE), BF16)], axis=0)
        readout = jnp.concatenate([readout, jnp.zeros((pad, STATE), BF16)], axis=0)
        step = jnp.concatenate([step, jnp.zeros((pad, HEADS), F32)], axis=0)
        small_s[f] = jnp.concatenate([inject, readout], axis=1)
        log_decay = -jnp.exp(alog_s_ref[...]) * step
        offset = jnp.zeros((8, HEADS), F32)
        for k in range(count):
            rows = pl.ds(k * CHUNK, CHUNK)
            part_k = slice(k * CHUNK, (k + 1) * CHUNK)
            cum = chunk_cumsum(log_decay[part_k])
            tail_k = jnp.exp(cum[CHUNK - 1 :, :] - cum) * step[part_k]
            tail_s[f, rows, :] = split3(tail_k)[:, : 2 * HEADS]
            grown_s[f, rows, :] = split3(jnp.exp(cum))
            both = widen(jnp.concatenate([jnp.exp(last_row(cum)), jnp.exp(offset)], axis=0), spread)
            rate_s[f, pl.ds(8 * k, 8), :] = both[:8]
            reach_s[f, pl.ds(8 * k, 8), :] = both[8:]
            offset = offset + last_row(cum)
            turned_s[k] = row_forms(cum, step[part_k])
            cum_s[...] = mm(split3(cum), spread[...])
            scores2 = masked_scores(readout[part_k], inject[part_k])
            for j in range(HEADS // 2):
                lanes = pl.ds(j * 128, 128)
                w_v[f, rows, lanes] = decay_weights(cum_s[:, lanes], turned_s.at[k], scores2, j, lane_low)
        tot_mine[f] = jnp.concatenate([offset, jnp.zeros((8, 128 - HEADS), F32)], axis=1)
        for half in range(halves):
            s = halves * f + half

            @pl.when(s != here)
            def _():
                tot_copy(s, here).start()

            @pl.when(s == here)
            def _():
                tot_got[here] = tot_mine[f]

        return carry

    lax.fori_loop(0, frames, home, 0)
    wo_load.start()
    wx_load.wait()

    def prepare_round(h):
        wait_bytes(tok_got.at[h], tok_recv.at[h])
        tail = rounded(nt(tok_got[h].reshape(total * HALF, D), wt[...]))
        small_t[0] = tail[:, : 2 * STATE]
        small_t[1] = jnp.concatenate(
            [tail[:, 4 * STATE :], jnp.zeros((total * HALF, 128 - 2 * HEADS), F32)], axis=1
        )
        rate = -jnp.exp(alog_t_ref[...])

        def prepare(q, carry):
            several = [q * TOGETHER + u for u in range(TOGETHER)]
            rows = [pl.ds(p, CHUNK, stride=HALF) for p in several]
            pairs = [small_t[0, r, :].astype(BF16) for r in rows]
            steps = [softplus(small_t[1, r, :][:, :HEADS] + bias_t_ref[...]) for r in rows]
            scores = [masked_scores(pair[:, STATE:], pair[:, :STATE]) for pair in pairs]
            cums = [chunk_cumsum(rate * step) for step in steps]
            forms = [row_forms(cum, step) for cum, step in zip(cums, steps)]
            for u, p in enumerate(several):
                scores_t[p] = scores[u]
                turned_t[p] = forms[u]
                cum3[p] = split3(cums[u])
            return carry

        lax.fori_loop(0, HALF // TOGETHER, prepare, 0)

    def take_totals():
        wait_bytes(tot_got.at[others], tot_recv)
        totals = jnp.concatenate([tot_got[s] for s in range(n_space)], axis=0)[:, :HEADS]
        growth[...] = widen(jnp.exp(totals), spread)
        wo_load.wait()

    def scan_group(g, h):
        x = rounded(nt(tok_got[h].reshape(total * HALF, D), wx[channels(g), :]))
        cum = mm(cum3[...].reshape(HALF * CHUNK, 3 * HEADS), spread[:, channels(g)])
        for jj in range(PAIRS):
            x_group[jj] = x[:, jj * 128 : (jj + 1) * 128]
            cum_group[jj] = cum[:, jj * 128 : (jj + 1) * 128]

        def item(q, inner):
            work = [(q * TOGETHER + u, jj) for u in range(TOGETHER) for jj in range(PAIRS)]
            weights = [
                decay_weights(
                    cum_group[jj, pl.ds(pl.multiple_of(p * CHUNK, CHUNK), CHUNK), :],
                    turned_t.at[p],
                    scores_t[p],
                    g * PAIRS + jj,
                    lane_low,
                )
                for p, jj in work
            ]
            inputs = [x_group[jj, pl.ds(p, CHUNK, stride=HALF), :] for p, jj in work]
            mixed = [mm(w, block_pair(x.astype(BF16))) for w, x in zip(weights, inputs)]
            for u, (p, jj) in enumerate(work):
                skip = skips[pl.ds(0, 1), pair_lanes(g * PAIRS + jj)]
                out_group[jj, pl.ds(p, CHUNK, stride=HALF), :] = mixed[u] + skip * inputs[u]
            return inner

        lax.fori_loop(0, HALF // TOGETHER, item, 0)
        for jj in range(PAIRS):
            leaving[h, g, :, :, pl.ds(jj * 128, 128)] = (
                out_group[jj].astype(BF16).reshape(total, HALF, 128)
            )

        def send(step, inner):
            ret_copy(lax.rem(me + step, n), me, g, h).start()
            return inner

        lax.fori_loop(1, n, send, 0)
        own_copy(g, h).start()

    def states(g):
        whole = lax.div(g, GROUP // NARROW)

        @pl.when(lax.rem(g, GROUP // NARROW) == 0)
        def _():
            wait_bytes(x_home.at[:, :, channels(whole)], ret_recv.at[whole])

        pieces = [(f, k, min(CHUNK, seq - k * CHUNK)) for f in range(frames) for k in range(count)]
        added = []
        for f, k, size in pieces:
            rows = pl.ds(k * CHUNK, size)
            tail_wide = mm(tail_s[f, rows, :], spread[: 2 * HEADS, narrow(g)])
            weighted = (x_home[f, rows, narrow(g)].astype(F32) * tail_wide).astype(BF16)
            added.append(tn(small_s[f, rows, :STATE], weighted))
        for f in range(frames):
            state = jnp.zeros((STATE, NARROW), F32)
            for k in range(count):
                starts[f, pl.ds(k * STATE, STATE), narrow(g)] = state.astype(BF16)
                state = rate_s[f, pl.ds(8 * k, 1), narrow(g)] * state + added[f * count + k]
            for half in range(halves):
                end[g, halves * f + half] = state[half * part : (half + 1) * part].astype(BF16)

        def send_state(step, carry):
            state_copy(lax.rem(here + step, n_space), here, g).start()
            return carry

        lax.fori_loop(1, n_space, send_state, 0)
        got[g, here] = end[g, here]

    def relay(g):
        wait_bytes(got.at[g, others], st_recv.at[g])
        running = jnp.zeros((part, NARROW), F32)
        for s in range(n_space):
            going[g, s] = running.astype(BF16)
            running = growth[pl.ds(8 * s, 1), narrow(g)] * running + got[g, s].astype(F32)

        def send_back(step, carry):
            back_copy(lax.rem(here + step, n_space), here, g).start()
            return carry

        lax.fori_loop(1, n_space, send_back, 0)
        entering[g, here] = going[g, here]

    def finish(g):
        wait_bytes(entering.at[g, others], back_recv.at[g])

        def frame(f):
            arrived = jnp.concatenate(
                [entering[g, halves * f + half] for half in range(halves)], axis=0
            ).astype(F32)
            sizes = [min(CHUNK, seq - k * CHUNK) for k in range(count)]
            carried, mixed = [], []
            for k, size in enumerate(sizes):
                rows = pl.ds(k * CHUNK, size)
                reach = reach_s[f, pl.ds(8 * k, 1), narrow(g)]
                state = starts[f, pl.ds(k * STATE, STATE), narrow(g)].astype(F32) + reach * arrived
                product = mm(small_s[f, rows, STATE:], state.astype(BF16))
                carried.append(product * mm(grown_s[f, rows, :], spread[:, narrow(g)]))
                for jj in range(NPAIRS):
                    lanes = pair_lanes(g * NPAIRS + jj)
                    full = x_home[f, rows, lanes]
                    if size < CHUNK:
                        full = jnp.concatenate([full, jnp.zeros((CHUNK - size, 128), BF16)], axis=0)
                    mixed.append(mm(w_v[f, rows, lanes], block_pair(full)))
            for k, size in enumerate(sizes):
                rows = pl.ds(k * CHUNK, size)
                energy = square[f, rows, :]
                for jj in range(NPAIRS):
                    lanes = pair_lanes(g * NPAIRS + jj)
                    y = mixed[k * NPAIRS + jj] + carried[k][:, jj * 128 : (jj + 1) * 128]
                    y = y + skips[pl.ds(8, 1), lanes] * x_home[f, rows, lanes].astype(F32)
                    z = z_v[f, rows, lanes].astype(F32)
                    y = y * (z * (1.0 / (1.0 + jnp.exp(-z))))
                    energy = energy + y * y
                    y_v[f, rows, pl.ds(jj * 128, 128)] = (y * gain_ref[:, lanes]).astype(BF16)
                square[f, rows, :] = energy

        for f in range(frames):
            frame(f)
        y_all = y_v[...].reshape(frames * seq, NARROW)
        acc[...] += mm(y_all, wz[narrow(g), :])

    @pl.when(me < holders)
    def _():
        def scan(i, carry):
            g = lax.rem(i, groups)
            h = i // groups

            @pl.when(g == 0)
            def _():
                prepare_round(h)

            scan_group(g, h)
            return carry

        lax.fori_loop(0, ROUNDS * groups, scan, 0)

    take_totals()

    def advance(i, carry):
        @pl.when(i < narrow_groups)
        def _():
            states(i)

        @pl.when(jnp.logical_and(i >= RELAY_LAG, i < narrow_groups + RELAY_LAG))
        def _():
            relay(i - RELAY_LAG)

        @pl.when(i >= FINISH_LAG)
        def _():
            finish(i - FINISH_LAG)

        return carry

    lax.fori_loop(0, narrow_groups + FINISH_LAG, advance, 0)

    def close(f, carry):
        mean = jnp.sum(square[f], axis=1, keepdims=True) * (1.0 / DI)
        scale = lax.rsqrt(mean + 1e-5)
        product = acc[pl.ds(pl.multiple_of(f * seq, 16), seq), :]
        out_ref[f] = (product * scale + tok_v[f].astype(F32)).astype(BF16)
        return carry

    lax.fori_loop(0, frames, close, 0)

    @pl.when(me < holders)
    def _():
        wait_bytes(tok_got.at[:, pl.ds(0, frames * (holders - 1))], tok_send)
        wait_bytes(leaving.at[:, :, pl.ds(0, frames * (n - 1))], ret_send)

    @pl.when(me >= holders)
    def _():
        wait_bytes(tok_got.at[:, pl.ds(0, frames * holders)], tok_send)

    wait_bytes(tot_got.at[others], tot_send)
    wait_bytes(end.at[:, others], st_send)
    wait_bytes(going.at[:, others], back_send)


def block(tok, w_turned, w_out, bias_t, alog_t, skip_t, bias_s, alog_s, skip_s, gain):
    n = lax.axis_size("tm")
    n_space = lax.axis_size("space")
    frames, seq = tok.shape[0], tok.shape[1]
    padded = -(-seq // CHUNK) * CHUNK
    count = padded // CHUNK
    total = n * frames
    groups = DI // GROUP
    part = frames * STATE // n_space
    tail = w_turned.shape[0] - 2 * DI
    anywhere = pl.BlockSpec(memory_space=pl.ANY)
    in_vmem = pl.BlockSpec(memory_space=pltpu.VMEM)
    dma = pltpu.SemaphoreType.DMA
    vmem = pltpu.VMEM
    return pl.pallas_call(
        functools.partial(block_kernel, n, n_space),
        out_shape=jax.ShapeDtypeStruct((frames, seq, D), BF16),
        in_specs=[anywhere] * 3 + [in_vmem] * 7,
        out_specs=in_vmem,
        scratch_shapes=[
            vmem((frames, seq, D), BF16),
            vmem((ROUNDS, total, HALF, D), BF16),
            vmem((DI, D), BF16),
            vmem((DI, D), BF16),
            vmem((tail, D), BF16),
            vmem((frames, seq, DI), BF16),
            vmem((frames, padded, DI), BF16),
            vmem((PAIRS, total * HALF, 128), F32),
            vmem((PAIRS, total * HALF, 128), F32),
            vmem((PAIRS, total * HALF, 128), F32),
            vmem((ROUNDS, groups, total, HALF, GROUP), BF16),
            vmem((2, total * HALF, 128), F32),
            vmem((HALF, 128, 128), F32),
            vmem((count, 128, 128), F32),
            vmem((HALF, CHUNK, 128), F32),
            vmem((HALF, CHUNK, 3 * HEADS), BF16),
            vmem((CHUNK, DI), F32),
            vmem((3 * HEADS, DI), BF16),
            vmem((16, DI), F32),
            vmem((frames, padded, 2 * STATE), BF16),
            vmem((frames, padded, 2 * HEADS), BF16),
            vmem((frames, padded, 3 * HEADS), BF16),
            vmem((frames, 8 * count, DI), F32),
            vmem((frames, 8 * count, DI), F32),
            vmem((frames, seq, DI), BF16),
            vmem((frames, 8, 128), F32),
            vmem((n_space, 8, 128), F32),
            vmem((n_space * 8, DI), F32),
            vmem((frames, count * STATE, DI), BF16),
            vmem((DI // NARROW, n_space, part, NARROW), BF16),
            vmem((DI // NARROW, n_space, part, NARROW), BF16),
            vmem((DI // NARROW, n_space, part, NARROW), BF16),
            vmem((DI // NARROW, n_space, part, NARROW), BF16),
            vmem((frames, seq, NARROW), BF16),
            vmem((frames, seq, 128), F32),
            vmem((frames * seq, D), F32),
            dma((5,)),
            dma(()),
            dma((ROUNDS,)),
            dma(()),
            dma((groups,)),
            dma(()),
            dma(()),
            dma(()),
            dma((DI // NARROW,)),
            dma(()),
            dma((DI // NARROW,)),
        ],
        compiler_params=pltpu.CompilerParams(
            collective_id=0, has_side_effects=True, vmem_limit_bytes=60 * MIB
        ),
    )(tok, w_turned, w_out, bias_t, alog_t, skip_t, bias_s, alog_s, skip_s, gain)


def body(
    tokens,
    w_in,
    w_out,
    a_log_time,
    a_log_space,
    dt_bias_time,
    dt_bias_space,
    skip_time,
    skip_space,
    norm_gain,
):
    frames = tokens.shape[0]
    tok = tokens.reshape(frames, -1, D)
    one = lambda v: v.reshape(1, -1)
    out = block(
        tok,
        w_in.T,
        w_out,
        one(dt_bias_time),
        one(a_log_time),
        one(skip_time),
        one(dt_bias_space),
        one(a_log_space),
        one(skip_space),
        one(norm_gain),
    )
    return out.reshape(tokens.shape)


def solution(mesh):
    placed = (P("tm", "space", None, None), P(), P(), P(), P(), P(), P(), P(), P(), P())
    return jax.shard_map(
        body, mesh=mesh, in_specs=placed, out_specs=P("tm", "space", None, None), check_vma=False
    )
```

```python
import functools

import jax
import jax.numpy as jnp
from jax import lax
from jax.experimental import pallas as pl
from jax.experimental.pallas import tpu as pltpu
from jax.sharding import PartitionSpec as P

D = 1024
HEADS = 32
HEAD_DIM = 64
STATE = 64
DI = 2048
CHUNK = 64
F32 = jnp.float32
BF16 = jnp.bfloat16
MIB = 1 << 20


def mm(a, b):
    return jnp.dot(a, b, preferred_element_type=F32)


def softplus(v):
    return jnp.maximum(v, 0.0) + jnp.log1p(jnp.exp(-jnp.abs(v)))


def split3(v):
    hi = v.astype(BF16)
    rest = v - hi.astype(F32)
    mid = rest.astype(BF16)
    low = (rest - mid.astype(F32)).astype(BF16)
    return jnp.concatenate([hi, mid, low], axis=1)


def head_spread():
    row = lax.broadcasted_iota(jnp.int32, (3 * HEADS, DI), 0) % HEADS
    col = lax.broadcasted_iota(jnp.int32, (3 * HEADS, DI), 1) // HEAD_DIM
    return (row == col).astype(BF16)


def causal_ones():
    row = lax.broadcasted_iota(jnp.int32, (CHUNK, CHUNK), 0)
    col = lax.broadcasted_iota(jnp.int32, (CHUNK, CHUNK), 1)
    return row >= col


def chunk_cumsum(log_decay):
    tri = causal_ones().astype(F32).astype(BF16)
    wide = mm(tri, split3(log_decay))
    return wide[:, :HEADS] + wide[:, HEADS : 2 * HEADS] + wide[:, 2 * HEADS :]


def row_forms(cum, step):
    pair = jnp.concatenate([cum, step, jnp.zeros((CHUNK, 2 * HEADS), F32)], axis=1)
    return jnp.concatenate([pair, pair], axis=0).T


def pair_rows(turned_ref, base, j, lane_low):
    even = turned_ref[pl.ds(base + 2 * j, 1), :]
    odd = turned_ref[pl.ds(base + 2 * j + 1, 1), :]
    return jnp.where(lane_low, even, odd)


def decay_weights(cum_wide, turned_ref, scores2, j, lane_low):
    cum_row = pair_rows(turned_ref, 0, j, lane_low)
    step_row = pair_rows(turned_ref, HEADS, j, lane_low)
    span = jnp.exp(jnp.minimum(cum_wide - cum_row, 0.0))
    return (span * (scores2 * step_row)).astype(BF16)


def masked_scores(readout, inject):
    scores = lax.dot_general(readout, inject, (((1,), (1,)), ((), ())), preferred_element_type=F32)
    scores = jnp.where(causal_ones(), scores, 0.0)
    return jnp.concatenate([scores, scores], axis=1)


def block_pair(x_pair):
    low = lax.broadcasted_iota(jnp.int32, x_pair.shape, 1) < HEAD_DIM
    zero = jnp.zeros_like(x_pair)
    return jnp.concatenate([jnp.where(low, x_pair, zero), jnp.where(low, zero, x_pair)], axis=0)


ITEMS = 16
GROUP = 256
PAIRS = GROUP // 128
TOGETHER = 8
NARROW = 256
RELAY_LAG = 2
FINISH_LAG = 4
NPAIRS = NARROW // 128
HALF = 8
ROUNDS = ITEMS // HALF


def nt(a, b):
    return lax.dot_general(a, b, (((1,), (1,)), ((), ())), preferred_element_type=F32)


def tn(a, b):
    return lax.dot_general(a, b, (((0,), (0,)), ((), ())), preferred_element_type=F32)


def rounded(v):
    return v.astype(BF16).astype(F32)


def widen(values, spread):
    return mm(split3(values), spread[...])


def last_row(values):
    return jnp.broadcast_to(values[CHUNK - 1 :, :], (8, HEADS))


def block_kernel(
    n,
    n_space,
    tok_hbm,
    w_hbm,
    wo_hbm,
    bias_t_ref,
    alog_t_ref,
    skip_t_ref,
    bias_s_ref,
    alog_s_ref,
    skip_s_ref,
    gain_ref,
    out_ref,
    tok_v,
    tok_got,
    wz,
    wx,
    wt,
    z_v,
    w_v,
    x_group,
    cum_group,
    out_group,
    leaving,
    small_t,
    turned_t,
    turned_s,
    scores_t,
    cum3,
    cum_s,
    spread,
    skips,
    small_s,
    tail_s,
    grown_s,
    rate_s,
    reach_s,
    x_home,
    tot_mine,
    tot_got,
    growth,
    starts,
    end,
    got,
    going,
    entering,
    y_v,
    square,
    acc,
    load_sem,
    tok_send,
    tok_recv,
    ret_send,
    ret_recv,
    tot_send,
    tot_recv,
    st_send,
    st_recv,
    back_send,
    back_recv,
):
    frames, seq = tok_v.shape[0], tok_v.shape[1]
    padded = w_v.shape[1]
    count = padded // CHUNK
    holders = seq // ITEMS
    total = n * frames
    groups = DI // GROUP
    narrow_groups = DI // NARROW
    halves = n_space // frames
    part = STATE // halves
    me = lax.axis_index("tm")
    here = lax.axis_index("space")

    tok_load = pltpu.make_async_copy(tok_hbm, tok_v, load_sem.at[0])
    wz_load = pltpu.make_async_copy(w_hbm.at[pl.ds(0, DI)], wz, load_sem.at[1])
    wt_load = pltpu.make_async_copy(w_hbm.at[pl.ds(2 * DI, wt.shape[0])], wt, load_sem.at[2])
    wx_load = pltpu.make_async_copy(w_hbm.at[pl.ds(DI, DI)], wx, load_sem.at[3])
    wo_load = pltpu.make_async_copy(wo_hbm, wz, load_sem.at[4])
    tok_load.start()
    wt_load.start()
    wz_load.start()
    wx_load.start()

    def remote(src, dst, send, recv, axis, device):
        return pltpu.make_async_remote_copy(
            src_ref=src,
            dst_ref=dst,
            send_sem=send,
            recv_sem=recv,
            device_id={axis: device},
            device_id_type=pl.DeviceIdType.MESH,
        )

    def frame_rows(d):
        return pl.ds(d * frames, frames)

    def channels(g):
        return pl.ds(pl.multiple_of(g * GROUP, GROUP), GROUP)

    def narrow(g):
        return pl.ds(pl.multiple_of(g * NARROW, NARROW), NARROW)

    def pair_lanes(j):
        return pl.ds(pl.multiple_of(j * 128, 128), 128)

    def block_of(d, h):
        return pl.ds(pl.multiple_of(d * ITEMS + h * HALF, HALF), HALF)

    def tok_copy(d, source, h):
        return remote(
            tok_hbm.at[:, block_of(d, h), :],
            tok_got.at[h, frame_rows(source)],
            tok_send,
            tok_recv.at[h],
            "tm",
            d,
        )

    def ret_copy(d, source, g, h):
        return remote(
            leaving.at[h, g, frame_rows(d)],
            x_home.at[:, block_of(source, h), channels(g)],
            ret_send,
            ret_recv.at[g],
            "tm",
            d,
        )

    def own_copy(g, h):
        return pltpu.make_async_copy(
            leaving.at[h, g, frame_rows(me)], x_home.at[:, block_of(me, h), channels(g)], ret_recv.at[g]
        )

    def own_tok(h):
        return pltpu.make_async_copy(
            tok_hbm.at[:, block_of(lax.rem(me, holders), h), :],
            tok_got.at[h, frame_rows(me)],
            tok_recv.at[h],
        )

    def tot_copy(s, slot):
        return remote(
            tot_mine.at[s // halves], tot_got.at[slot], tot_send, tot_recv, "space", s
        )

    def state_copy(s, slot, g):
        return remote(
            end.at[g, s], got.at[g, slot], st_send, st_recv.at[g], "space", s
        )

    def back_copy(s, slot, g):
        return remote(
            going.at[g, s], entering.at[g, slot], back_send, back_recv.at[g], "space", s
        )

    def wait_bytes(ref, sem):
        pltpu.make_async_copy(ref, ref, sem).wait()

    others = pl.ds(0, n_space - 1)
    barrier = pltpu.get_barrier_semaphore()
    for step in range(1, n):
        pl.semaphore_signal(
            barrier,
            inc=1,
            device_id={"tm": lax.rem(me + step, n)},
            device_id_type=pl.DeviceIdType.MESH,
        )
    for step in range(1, n_space):
        pl.semaphore_signal(
            barrier,
            inc=1,
            device_id={"space": lax.rem(here + step, n_space)},
            device_id_type=pl.DeviceIdType.MESH,
        )
    pl.semaphore_wait(barrier, n + n_space - 2)

    def send_tokens(i, carry):
        h = i // (n - 1)
        d = lax.rem(me + 1 + lax.rem(i, n - 1), n)

        @pl.when(d < holders)
        def _():
            tok_copy(d, me, h).start()

        return carry

    lax.fori_loop(0, ROUNDS * (n - 1), send_tokens, 0)

    @pl.when(me < holders)
    def _():
        for h in range(ROUNDS):
            own_tok(h).start()

    spread[...] = head_spread()
    skips[...] = widen(
        jnp.concatenate(
            [
                jnp.broadcast_to(skip_t_ref[...], (8, HEADS)),
                jnp.broadcast_to(skip_s_ref[...], (8, HEADS)),
            ],
            axis=0,
        ),
        spread,
    )
    square[...] = jnp.zeros_like(square)
    acc[...] = jnp.zeros_like(acc)
    lane_low = lax.broadcasted_iota(jnp.int32, (1, 2 * CHUNK), 1) < CHUNK
    tok_load.wait()
    wt_load.wait()
    wz_load.wait()

    def home(f, carry):
        tok = tok_v[f]
        z_v[f] = nt(tok, wz[...]).astype(BF16)
        tail = nt(tok, wt[...])
        inject = tail[:, 2 * STATE : 3 * STATE].astype(BF16)
        readout = tail[:, 3 * STATE : 4 * STATE].astype(BF16)
        step = softplus(tail[:, 4 * STATE + HEADS : 4 * STATE + 2 * HEADS] + bias_s_ref[...])
        pad = padded - seq
        inject = jnp.concatenate([inject, jnp.zeros((pad, STATE), BF16)], axis=0)
        readout = jnp.concatenate([readout, jnp.zeros((pad, STATE), BF16)], axis=0)
        step = jnp.concatenate([step, jnp.zeros((pad, HEADS), F32)], axis=0)
        small_s[f] = jnp.concatenate([inject, readout], axis=1)
        log_decay = -jnp.exp(alog_s_ref[...]) * step
        offset = jnp.zeros((8, HEADS), F32)
        for k in range(count):
            rows = pl.ds(k * CHUNK, CHUNK)
            part_k = slice(k * CHUNK, (k + 1) * CHUNK)
            cum = chunk_cumsum(log_decay[part_k])
            tail_k = jnp.exp(cum[CHUNK - 1 :, :] - cum) * step[part_k]
            tail_s[f, rows, :] = split3(tail_k)[:, : 2 * HEADS]
            grown_s[f, rows, :] = split3(jnp.exp(cum))
            both = widen(jnp.concatenate([jnp.exp(last_row(cum)), jnp.exp(offset)], axis=0), spread)
            rate_s[f, pl.ds(8 * k, 8), :] = both[:8]
            reach_s[f, pl.ds(8 * k, 8), :] = both[8:]
            offset = offset + last_row(cum)
            turned_s[k] = row_forms(cum, step[part_k])
            cum_s[...] = mm(split3(cum), spread[...])
            scores2 = masked_scores(readout[part_k], inject[part_k])
            for j in range(HEADS // 2):
                lanes = pl.ds(j * 128, 128)
                w_v[f, rows, lanes] = decay_weights(cum_s[:, lanes], turned_s.at[k], scores2, j, lane_low)
        tot_mine[f] = jnp.concatenate([offset, jnp.zeros((8, 128 - HEADS), F32)], axis=1)
        for half in range(halves):
            s = halves * f + half

            @pl.when(s != here)
            def _():
                tot_copy(s, here).start()

            @pl.when(s == here)
            def _():
                tot_got[here] = tot_mine[f]

        return carry

    lax.fori_loop(0, frames, home, 0)
    wo_load.start()
    wx_load.wait()

    def prepare_round(h):
        wait_bytes(tok_got.at[h], tok_recv.at[h])
        tail = rounded(nt(tok_got[h].reshape(total * HALF, D), wt[...]))
        small_t[0] = tail[:, : 2 * STATE]
        small_t[1] = jnp.concatenate(
            [tail[:, 4 * STATE :], jnp.zeros((total * HALF, 128 - 2 * HEADS), F32)], axis=1
        )
        rate = -jnp.exp(alog_t_ref[...])

        def prepare(q, carry):
            several = [q * TOGETHER + u for u in range(TOGETHER)]
            rows = [pl.ds(p, CHUNK, stride=HALF) for p in several]
            pairs = [small_t[0, r, :].astype(BF16) for r in rows]
            steps = [softplus(small_t[1, r, :][:, :HEADS] + bias_t_ref[...]) for r in rows]
            scores = [masked_scores(pair[:, STATE:], pair[:, :STATE]) for pair in pairs]
            cums = [chunk_cumsum(rate * step) for step in steps]
            forms = [row_forms(cum, step) for cum, step in zip(cums, steps)]
            for u, p in enumerate(several):
                scores_t[p] = scores[u]
                turned_t[p] = forms[u]
                cum3[p] = split3(cums[u])
            return carry

        lax.fori_loop(0, HALF // TOGETHER, prepare, 0)

    def take_totals():
        wait_bytes(tot_got.at[others], tot_recv)
        totals = jnp.concatenate([tot_got[s] for s in range(n_space)], axis=0)[:, :HEADS]
        growth[...] = widen(jnp.exp(totals), spread)
        wo_load.wait()

    def scan_group(g, h):
        x = rounded(nt(tok_got[h].reshape(total * HALF, D), wx[channels(g), :]))
        cum = mm(cum3[...].reshape(HALF * CHUNK, 3 * HEADS), spread[:, channels(g)])
        for jj in range(PAIRS):
            x_group[jj] = x[:, jj * 128 : (jj + 1) * 128]
            cum_group[jj] = cum[:, jj * 128 : (jj + 1) * 128]

        def item(q, inner):
            work = [(q * TOGETHER + u, jj) for u in range(TOGETHER) for jj in range(PAIRS)]
            weights = [
                decay_weights(
                    cum_group[jj, pl.ds(pl.multiple_of(p * CHUNK, CHUNK), CHUNK), :],
                    turned_t.at[p],
                    scores_t[p],
                    g * PAIRS + jj,
                    lane_low,
                )
                for p, jj in work
            ]
            inputs = [x_group[jj, pl.ds(p, CHUNK, stride=HALF), :] for p, jj in work]
            mixed = [mm(w, block_pair(x.astype(BF16))) for w, x in zip(weights, inputs)]
            for u, (p, jj) in enumerate(work):
                skip = skips[pl.ds(0, 1), pair_lanes(g * PAIRS + jj)]
                out_group[jj, pl.ds(p, CHUNK, stride=HALF), :] = mixed[u] + skip * inputs[u]
            return inner

        lax.fori_loop(0, HALF // TOGETHER, item, 0)
        for jj in range(PAIRS):
            leaving[h, g, :, :, pl.ds(jj * 128, 128)] = (
                out_group[jj].astype(BF16).reshape(total, HALF, 128)
            )

        def send(step, inner):
            ret_copy(lax.rem(me + step, n), me, g, h).start()
            return inner

        lax.fori_loop(1, n, send, 0)
        own_copy(g, h).start()

    def states(g):
        whole = lax.div(g, GROUP // NARROW)

        @pl.when(lax.rem(g, GROUP // NARROW) == 0)
        def _():
            wait_bytes(x_home.at[:, :, channels(whole)], ret_recv.at[whole])

        pieces = [(f, k, min(CHUNK, seq - k * CHUNK)) for f in range(frames) for k in range(count)]
        added = []
        for f, k, size in pieces:
            rows = pl.ds(k * CHUNK, size)
            tail_wide = mm(tail_s[f, rows, :], spread[: 2 * HEADS, narrow(g)])
            weighted = (x_home[f, rows, narrow(g)].astype(F32) * tail_wide).astype(BF16)
            added.append(tn(small_s[f, rows, :STATE], weighted))
        for f in range(frames):
            state = jnp.zeros((STATE, NARROW), F32)
            for k in range(count):
                starts[f, pl.ds(k * STATE, STATE), narrow(g)] = state.astype(BF16)
                state = rate_s[f, pl.ds(8 * k, 1), narrow(g)] * state + added[f * count + k]
            for half in range(halves):
                end[g, halves * f + half] = state[half * part : (half + 1) * part].astype(BF16)

        def send_state(step, carry):
            state_copy(lax.rem(here + step, n_space), here, g).start()
            return carry

        lax.fori_loop(1, n_space, send_state, 0)
        got[g, here] = end[g, here]

    def relay(g):
        wait_bytes(got.at[g, others], st_recv.at[g])
        running = jnp.zeros((part, NARROW), F32)
        for s in range(n_space):
            going[g, s] = running.astype(BF16)
            running = growth[pl.ds(8 * s, 1), narrow(g)] * running + got[g, s].astype(F32)

        def send_back(step, carry):
            back_copy(lax.rem(here + step, n_space), here, g).start()
            return carry

        lax.fori_loop(1, n_space, send_back, 0)
        entering[g, here] = going[g, here]

    def finish(g):
        wait_bytes(entering.at[g, others], back_recv.at[g])

        def frame(f):
            arrived = jnp.concatenate(
                [entering[g, halves * f + half] for half in range(halves)], axis=0
            ).astype(F32)
            sizes = [min(CHUNK, seq - k * CHUNK) for k in range(count)]
            carried, mixed = [], []
            for k, size in enumerate(sizes):
                rows = pl.ds(k * CHUNK, size)
                reach = reach_s[f, pl.ds(8 * k, 1), narrow(g)]
                state = starts[f, pl.ds(k * STATE, STATE), narrow(g)].astype(F32) + reach * arrived
                product = mm(small_s[f, rows, STATE:], state.astype(BF16))
                carried.append(product * mm(grown_s[f, rows, :], spread[:, narrow(g)]))
                for jj in range(NPAIRS):
                    lanes = pair_lanes(g * NPAIRS + jj)
                    full = x_home[f, rows, lanes]
                    if size < CHUNK:
                        full = jnp.concatenate([full, jnp.zeros((CHUNK - size, 128), BF16)], axis=0)
                    mixed.append(mm(w_v[f, rows, lanes], block_pair(full)))
            for k, size in enumerate(sizes):
                rows = pl.ds(k * CHUNK, size)
                energy = square[f, rows, :]
                for jj in range(NPAIRS):
                    lanes = pair_lanes(g * NPAIRS + jj)
                    y = mixed[k * NPAIRS + jj] + carried[k][:, jj * 128 : (jj + 1) * 128]
                    y = y + skips[pl.ds(8, 1), lanes] * x_home[f, rows, lanes].astype(F32)
                    z = z_v[f, rows, lanes].astype(F32)
                    y = y * (z * (1.0 / (1.0 + jnp.exp(-z))))
                    energy = energy + y * y
                    y_v[f, rows, pl.ds(jj * 128, 128)] = (y * gain_ref[:, lanes]).astype(BF16)
                square[f, rows, :] = energy

        for f in range(frames):
            frame(f)
        y_all = y_v[...].reshape(frames * seq, NARROW)
        acc[...] += mm(y_all, wz[narrow(g), :])

    @pl.when(me < holders)
    def _():
        def scan(i, carry):
            g = lax.rem(i, groups)
            h = i // groups

            @pl.when(g == 0)
            def _():
                prepare_round(h)

            scan_group(g, h)
            return carry

        lax.fori_loop(0, ROUNDS * groups, scan, 0)

    take_totals()

    def advance(i, carry):
        @pl.when(i < narrow_groups)
        def _():
            states(i)

        @pl.when(jnp.logical_and(i >= RELAY_LAG, i < narrow_groups + RELAY_LAG))
        def _():
            relay(i - RELAY_LAG)

        @pl.when(i >= FINISH_LAG)
        def _():
            finish(i - FINISH_LAG)

        return carry

    lax.fori_loop(0, narrow_groups + FINISH_LAG, advance, 0)

    def close(f, carry):
        mean = jnp.sum(square[f], axis=1, keepdims=True) * (1.0 / DI)
        scale = lax.rsqrt(mean + 1e-5)
        product = acc[pl.ds(pl.multiple_of(f * seq, 16), seq), :]
        out_ref[f] = (product * scale + tok_v[f].astype(F32)).astype(BF16)
        return carry

    lax.fori_loop(0, frames, close, 0)

    @pl.when(me < holders)
    def _():
        wait_bytes(tok_got.at[:, pl.ds(0, frames * (holders - 1))], tok_send)
        wait_bytes(leaving.at[:, :, pl.ds(0, frames * (n - 1))], ret_send)

    @pl.when(me >= holders)
    def _():
        wait_bytes(tok_got.at[:, pl.ds(0, frames * holders)], tok_send)

    wait_bytes(tot_got.at[others], tot_send)
    wait_bytes(end.at[:, others], st_send)
    wait_bytes(going.at[:, others], back_send)


def block(tok, w_turned, w_out, bias_t, alog_t, skip_t, bias_s, alog_s, skip_s, gain):
    n = lax.axis_size("tm")
    n_space = lax.axis_size("space")
    frames, seq = tok.shape[0], tok.shape[1]
    padded = -(-seq // CHUNK) * CHUNK
    count = padded // CHUNK
    total = n * frames
    groups = DI // GROUP
    part = frames * STATE // n_space
    tail = w_turned.shape[0] - 2 * DI
    anywhere = pl.BlockSpec(memory_space=pl.ANY)
    in_vmem = pl.BlockSpec(memory_space=pltpu.VMEM)
    dma = pltpu.SemaphoreType.DMA
    vmem = pltpu.VMEM
    return pl.pallas_call(
        functools.partial(block_kernel, n, n_space),
        out_shape=jax.ShapeDtypeStruct((frames, seq, D), BF16),
        in_specs=[anywhere] * 3 + [in_vmem] * 7,
        out_specs=in_vmem,
        scratch_shapes=[
            vmem((frames, seq, D), BF16),
            vmem((ROUNDS, total, HALF, D), BF16),
            vmem((DI, D), BF16),
            vmem((DI, D), BF16),
            vmem((tail, D), BF16),
            vmem((frames, seq, DI), BF16),
            vmem((frames, padded, DI), BF16),
            vmem((PAIRS, total * HALF, 128), F32),
            vmem((PAIRS, total * HALF, 128), F32),
            vmem((PAIRS, total * HALF, 128), F32),
            vmem((ROUNDS, groups, total, HALF, GROUP), BF16),
            vmem((2, total * HALF, 128), F32),
            vmem((HALF, 128, 128), F32),
            vmem((count, 128, 128), F32),
            vmem((HALF, CHUNK, 128), F32),
            vmem((HALF, CHUNK, 3 * HEADS), BF16),
            vmem((CHUNK, DI), F32),
            vmem((3 * HEADS, DI), BF16),
            vmem((16, DI), F32),
            vmem((frames, padded, 2 * STATE), BF16),
            vmem((frames, padded, 2 * HEADS), BF16),
            vmem((frames, padded, 3 * HEADS), BF16),
            vmem((frames, 8 * count, DI), F32),
            vmem((frames, 8 * count, DI), F32),
            vmem((frames, seq, DI), BF16),
            vmem((frames, 8, 128), F32),
            vmem((n_space, 8, 128), F32),
            vmem((n_space * 8, DI), F32),
            vmem((frames, count * STATE, DI), BF16),
            vmem((DI // NARROW, n_space, part, NARROW), BF16),
            vmem((DI // NARROW, n_space, part, NARROW), BF16),
            vmem((DI // NARROW, n_space, part, NARROW), BF16),
            vmem((DI // NARROW, n_space, part, NARROW), BF16),
            vmem((frames, seq, NARROW), BF16),
            vmem((frames, seq, 128), F32),
            vmem((frames * seq, D), F32),
            dma((5,)),
            dma(()),
            dma((ROUNDS,)),
            dma(()),
            dma((groups,)),
            dma(()),
            dma(()),
            dma(()),
            dma((DI // NARROW,)),
            dma(()),
            dma((DI // NARROW,)),
        ],
        compiler_params=pltpu.CompilerParams(
            collective_id=0, has_side_effects=True, vmem_limit_bytes=60 * MIB
        ),
    )(tok, w_turned, w_out, bias_t, alog_t, skip_t, bias_s, alog_s, skip_s, gain)


def body(
    tokens,
    w_in,
    w_out,
    a_log_time,
    a_log_space,
    dt_bias_time,
    dt_bias_space,
    skip_time,
    skip_space,
    norm_gain,
):
    frames = tokens.shape[0]
    tok = tokens.reshape(frames, -1, D)
    one = lambda v: v.reshape(1, -1)
    out = block(
        tok,
        w_in.T,
        w_out,
        one(dt_bias_time),
        one(a_log_time),
        one(skip_time),
        one(dt_bias_space),
        one(a_log_space),
        one(skip_space),
        one(norm_gain),
    )
    return out.reshape(tokens.shape)


def solution(mesh):
    placed = (P("tm", "space", None, None), P(), P(), P(), P(), P(), P(), P(), P(), P())
    return jax.shard_map(
        body, mesh=mesh, in_specs=placed, out_specs=P("tm", "space", None, None), check_vma=False
    )
```
